512 devices in a mesh: seq: 8 (over x, core), tok: 64 (over z, y).
Axes of the slice: x: 4, y: 4, z: 16, core: 2. Of those that a mesh axis runs over, the one named last changes fastest.
Arguments:
- block_in: bfloat16 [8, 256, 1024], P('seq'), may hold values from -6 to 6
- accept: int32 [2, 8, 256], P(None, 'seq'), may hold values 0 or 1
- cache_len: int32 [8], P('seq'), may hold values from 8192 to 16384, as said below
- slot_page: int32 [8, 192], P('seq', 'tok'), may hold values from -1 to 127, as said below
- cache_kv: bfloat16 [8, 192, 128, 2048], P('seq', 'tok'), as said below
- w_query: bfloat16 [1024, 1024], P('seq', 'tok'), may hold values from -0.25 to 0.25
- w_key_value: bfloat16 [1024, 2048], P('seq', 'tok'), may hold values from -0.375 to 0.375
- w_out: bfloat16 [1024, 1024], P('seq', 'tok'), may hold values from -0.1875 to 0.1875
- gain_attn: float32 [1024], replicated, may hold values from 0.1 to 1.9
- w_up: bfloat16 [1024, 4096], P('seq', 'tok'), may hold values from -0.1875 to 0.1875
- w_down: bfloat16 [4096, 1024], P('tok', 'seq'), may hold values from -0.09375 to 0.09375
- gain_mlp: float32 [1024], replicated, may hold values from 0.1 to 1.9
Outputs:
- refined: bfloat16 [8, 256, 1024], P('seq')
The draws below stay inside these ranges and needn't reach their ends.
Inputs may be any that keep to these rules, and one draw needn't show every extreme that they name: `cache_len`: one sequence has exactly 16384 cached tokens. `slot_page`: slots j * 3 to (j + 1) * 3 - 1 of a row are those of index j of tok. Each page 0 to ceil(cache_len[s] / 128) - 1 of sequence s is in exactly one slot of row s, every other slot holds -1, and in every row some index of tok has all 3 of its slots filled. `cache_kv`: finite values; entries of empty slots are arbitrary.
All inputs are finite; a program needn't handle non-finite values. No bound on the sum of `accept` on one device may be relied on, other than what follows from the above.
Results may differ from the reference program's by a relative error of at most 0.035.
The reference program's roundings to bfloat16 on the way (of `weights`, `attention`, `settled`, `hidden` and `second_in`) count: a program that leaves them out, or rounds other values in their place, can miss the bound.
Values may be sent and summed in bfloat16 or wider, within the bound.
A program may use at most 64 MiB of HBM per device.

```python
import jax
import jax.numpy as jnp
from jax import lax

D = 1024
HEADS = 16
HEAD_DIM = 64
FF = 4096
BLOCK = 256
PAGE = 128
CACHE_MAX = 16384
SEQS = 8
TOK_DEV = 4
PAGES = 128
SLOTS = 3
POOL = 192
N_TOK = 64


def cache_layout(key):
    base_key = jax.random.fold_in(key, 7)
    len_key, page_key = jax.random.split(base_key, 2)
    lengths = jax.random.randint(len_key, (SEQS,), CACHE_MAX // 2, CACHE_MAX + 1).astype(jnp.int32)
    longest = jax.random.randint(jax.random.fold_in(len_key, 3), (), 0, SEQS)
    seq_ids = jnp.arange(SEQS, dtype=jnp.int32)
    if SEQS > 2:
        shortest = (longest + 1) % SEQS
        lengths = jnp.where(seq_ids == shortest, CACHE_MAX // 2, lengths)
    lengths = jnp.where(seq_ids == longest, CACHE_MAX, lengths).astype(jnp.int32)
    live_pages = (lengths + PAGE - 1) // PAGE

    def assign_pages(seq_key, live_count):
        hot_key, slot_key, order_key = jax.random.split(seq_key, 3)
        hot_device = jax.random.randint(hot_key, (), 0, N_TOK)
        slot_ids = jnp.arange(POOL, dtype=jnp.int32)
        slot_rank = jax.random.permutation(slot_key, POOL).astype(jnp.int32)
        priority = jnp.where(slot_ids // SLOTS == hot_device, slot_ids % SLOTS, SLOTS + slot_rank)
        fill_order = jnp.argsort(priority).astype(jnp.int32)
        page_ids = jnp.arange(PAGES, dtype=jnp.int32)
        page_rank = jax.random.permutation(order_key, PAGES).astype(jnp.int32)
        page_order = jnp.argsort(jnp.where(page_ids < live_count, page_rank, PAGES + page_rank)).astype(jnp.int32)
        assigned = jnp.where(page_ids < live_count, page_order, -1).astype(jnp.int32)
        assigned = jnp.concatenate([assigned, jnp.full((POOL - PAGES,), -1, jnp.int32)])
        return jnp.zeros((POOL,), jnp.int32).at[fill_order].set(assigned)
    slot_table = jax.vmap(assign_pages)(jax.random.split(page_key, SEQS), live_pages)
    return (lengths, slot_table)


def draw_cache_len(key, part):
    lengths, slot_table = cache_layout(key)
    return lengths


def draw_slot_page(key, part):
    lengths, slot_table = cache_layout(key)
    return slot_table


def draw_cache_kv(key, part):
    array_shape = (SEQS, POOL, PAGE, 2 * D)
    drawn_draw = 2.0 * jax.random.truncated_normal(key, -4.0, 4.0, array_shape, jnp.float32)
    return drawn_draw.astype(jnp.bfloat16)


def touch_ends(result, rng, low, largest):
    extent = result.shape
    spot = [jax.random.randint(jax.random.fold_in(rng, axis), (), 0, extent[axis]) for axis in range(len(extent))]
    result = result.at[tuple(spot)].set(low)
    longest = extent.index(max(extent))
    spot[longest] = (spot[longest] + 1) % extent[longest]
    return result.at[tuple(spot)].set(largest)


def level_of(stream_key, extent, cuts, smallest, high):
    level, own = 1.0, jax.random.fold_in(stream_key, 6)
    for axis_at, parts in cuts:
        heights = jnp.exp(jax.random.uniform(jax.random.fold_in(own, axis_at), (parts,), jnp.float32, smallest / len(cuts), high / len(cuts)))
        level = level * jnp.repeat(heights, extent[axis_at] // parts).reshape([-1 if axis == axis_at else 1 for axis in range(len(extent))])
    return level


def centred(rng, extent, spread, most, pieces=(), held_as=jnp.bfloat16):
    result = jax.random.normal(rng, extent, jnp.float32) * spread
    if len(pieces) > 0:
        result = level_of(rng, extent, pieces, -0.22, 0.18) * result
    return jnp.clip(result, min=-most, max=most).astype(held_as)


def setup_inputs(seed: int = 0) -> dict:
    streams_of = jax.random.split(jax.random.key(seed), 13)
    block_in = centred(streams_of[0], (SEQS, BLOCK, D), 1.0, 6.0, ((0, 8),))
    accept = touch_ends((jax.random.randint(streams_of[1], (2, SEQS, BLOCK), 0, 2) < 1).astype(jnp.int32), jax.random.fold_in(streams_of[1], 1), 0, 1)
    cache_len = draw_cache_len(jax.random.fold_in(streams_of[12], 71), 0)
    slot_page = draw_slot_page(jax.random.fold_in(streams_of[12], 71), 0)
    cache_kv = draw_cache_kv(jax.random.fold_in(streams_of[12], 71), 0)
    w_query = centred(streams_of[5], (D, D), (D * 4 // 9) ** -0.5, 0.25, ((0, 8), (1, 64)))
    w_key_value = centred(streams_of[6], (D, 2 * D), (D // 4) ** -0.5, 0.375, ((0, 8), (1, 64)))
    w_out = centred(streams_of[7], (D, D), D ** -0.5, 0.1875, ((0, 8), (1, 64)))
    gain_attn = jnp.clip(1.0 + 0.18 * jax.random.normal(streams_of[8], (D,), jnp.float32), 0.1, 1.9)
    w_up = centred(streams_of[9], (D, FF), D ** -0.5, 0.1875, ((0, 8), (1, 64)))
    w_down = centred(streams_of[10], (FF, D), FF ** -0.5, 0.09375, ((0, 64), (1, 8)))
    gain_mlp = jnp.clip(1.0 + 0.18 * jax.random.normal(streams_of[11], (D,), jnp.float32), 0.1, 1.9)
    return {"block_in": block_in, "accept": accept, "cache_len": cache_len, "slot_page": slot_page, "cache_kv": cache_kv, "w_query": w_query, "w_key_value": w_key_value, "w_out": w_out, "gain_attn": gain_attn, "w_up": w_up, "w_down": w_down, "gain_mlp": gain_mlp}


EPSILON = 1e-05
FLOOR_SCORE = -1e+30

def layer_norm(values, gain_vec):
    average = lax.optimization_barrier(jnp.mean(values, axis=-1, keepdims=True))
    centered = values - average
    variance = lax.optimization_barrier(jnp.mean(centered * centered, axis=-1, keepdims=True))
    return centered * lax.rsqrt(variance + EPSILON) * gain_vec

def merge_state(earlier, later):
    overall = jnp.maximum(earlier[0], later[0])
    early_factor = jnp.exp(earlier[0] - overall)
    late_factor = jnp.exp(later[0] - overall)
    totals = earlier[1] * early_factor + later[1] * late_factor
    weighted = earlier[2] * early_factor[..., None] + later[2] * late_factor[..., None]
    return (overall, totals, weighted)

def page_partial(queries, page_keys, page_values, usable):
    scores = jnp.einsum('sqhe,skhe->sqhk', queries.astype(jnp.float32), page_keys.astype(jnp.float32)) * HEAD_DIM ** (-0.5)
    masked = jnp.where(usable[:, None, None, :], scores, FLOOR_SCORE)
    peaks = lax.optimization_barrier(jnp.max(masked, axis=-1))
    weights = jnp.where(usable[:, None, None, :], jnp.exp(masked - peaks[..., None]), 0.0).astype(jnp.bfloat16)
    weights = lax.optimization_barrier(weights).astype(jnp.float32)
    weighted = jnp.einsum('sqhk,skhe->sqhe', weights, page_values.astype(jnp.float32))
    totals = lax.optimization_barrier(jnp.sum(weights, axis=-1))
    return (peaks, totals, weighted)

def reference(block_in, accept, cache_len, slot_page, cache_kv, w_query, w_key_value, w_out, gain_attn, w_up, w_down, gain_mlp):
    seq_ids = jnp.arange(SEQS, dtype=jnp.int32)
    slot_ids = jnp.broadcast_to(jnp.arange(POOL, dtype=jnp.int32)[None, :], (SEQS, POOL))
    targets = jnp.where(slot_page >= 0, slot_page, PAGES).astype(jnp.int32)
    slot_of_page = jnp.zeros((SEQS, PAGES + 1), jnp.int32).at[seq_ids[:, None], targets].set(slot_ids)[:, :PAGES]
    offsets = jnp.arange(PAGE, dtype=jnp.int32)

    def attend(inputs):
        flat_rows = inputs.reshape(SEQS * BLOCK, D)
        queries = jnp.dot(flat_rows, w_query, preferred_element_type=jnp.float32).astype(jnp.bfloat16)
        queries = queries.reshape(SEQS, BLOCK, HEADS, HEAD_DIM)
        key_value = jnp.dot(flat_rows, w_key_value, preferred_element_type=jnp.float32).astype(jnp.bfloat16)
        block_keys = key_value[:, :D].reshape(SEQS, N_TOK, TOK_DEV, HEADS, HEAD_DIM).astype(jnp.float32)
        block_values = key_value[:, D:].reshape(SEQS, N_TOK, TOK_DEV, HEADS, HEAD_DIM).astype(jnp.float32)
        scores = jnp.einsum('sqhe,sgkhe->sqhgk', queries.astype(jnp.float32), block_keys) * HEAD_DIM ** (-0.5)
        group_peaks = lax.optimization_barrier(jnp.max(scores, axis=-1))
        weights = jnp.exp(scores - group_peaks[..., None]).astype(jnp.bfloat16)
        weights = lax.optimization_barrier(weights).astype(jnp.float32)
        overall = lax.optimization_barrier(jnp.max(group_peaks, axis=-1))
        factor = jnp.exp(group_peaks - overall[..., None])
        scaled = weights * factor[..., None]
        weighted = jnp.einsum('sqhgk,sgkhe->sqhe', scaled, block_values)
        totals = lax.optimization_barrier(jnp.sum(scaled, axis=(-2, -1)))
        carry_state = (overall, totals, weighted)

        def page_step(carry_state, page_no):
            slot_now = slot_of_page[:, page_no]
            page_pair = cache_kv[seq_ids, slot_now]
            positions = page_no * PAGE + offsets
            usable = positions[None, :] < cache_len[:, None]
            page_keys = page_pair[..., :D].reshape(SEQS, PAGE, HEADS, HEAD_DIM)
            page_values = page_pair[..., D:].reshape(SEQS, PAGE, HEADS, HEAD_DIM)
            partial_value = page_partial(queries, page_keys, page_values, usable)
            return (merge_state(carry_state, partial_value), page_no)
        carry_state, unused = lax.scan(page_step, carry_state, jnp.arange(PAGES, dtype=jnp.int32))
        overall, totals, weighted = carry_state
        attention = (weighted / totals[..., None]).astype(jnp.bfloat16).reshape(SEQS * BLOCK, D)
        residual = flat_rows.astype(jnp.float32) + jnp.dot(attention, w_out, preferred_element_type=jnp.float32)
        return layer_norm(residual, gain_attn).astype(jnp.bfloat16)

    def feed(settled):
        hidden = jax.nn.gelu(jnp.dot(settled, w_up, preferred_element_type=jnp.float32), approximate=False).astype(jnp.bfloat16)
        projected = jnp.dot(hidden, w_down, preferred_element_type=jnp.float32)
        return layer_norm(settled.astype(jnp.float32) + projected, gain_mlp).astype(jnp.bfloat16).reshape(SEQS, BLOCK, D)
    first_out = feed(attend(block_in))
    second_in = jnp.where(accept[0][..., None] == 1, first_out, block_in)
    second_out = feed(attend(second_in))
    return jnp.where(accept[1][..., None] == 1, second_out, second_in)
```

```python
import jax
import jax.numpy as jnp
from jax import lax
from jax.experimental import pallas as pl
from jax.experimental.pallas import tpu as pltpu
from jax.sharding import PartitionSpec as P

MESH = pl.DeviceIdType.MESH
BF = jnp.bfloat16
F32 = jnp.float32

D = 1024
TOK = 256
NZ, NY, NX = 16, 4, 4
ROWS = TOK // NZ
KEYS = 384
EPSILON = 1e-05
FLOOR_SCORE = -1e30
MASKED = -3e38

(WS, AZ, KVY, OY, QX, KVX, OX, QC, KVC, OC, UZ, DZ, UX, DX, UC, DC) = range(16)
(GQZ, GQY, RSY, RSYM, RSZ, RSZM, GAY, GOY, RFY) = range(9)
FIN_Z, FIN_Y = 34, 35
N_SEM = 36


def dot_nn(a, b):
    return lax.dot_general(a, b, (((1,), (0,)), ((), ())), preferred_element_type=F32)


def dot_nt(a, b):
    return lax.dot_general(a, b, (((1,), (1,)), ((), ())), preferred_element_type=F32)


def layer_norm(values, gain):
    average = jnp.mean(values, axis=-1, keepdims=True)
    centered = values - average
    variance = jnp.mean(centered * centered, axis=-1, keepdims=True)
    return centered * lax.rsqrt(variance + EPSILON) * gain


def kernel(
    x_ref, accept_ref, len_ref, page_ref, cache_ref, wq_ref, wkv_ref, wo_ref, wu_ref, wd_ref, ga_ref, gm_ref,
    out_ref,
    kv_c, vt, ws, az, qw, kvw, ow, up, down,
    q_own, qz, qt, ot, ml, ry, rym, tz, ml2, rz, rzm, wt, att, ob, fp, fin, fz,
    ssem, rsem, lsem,
):
    s, t = lax.axis_index("seq"), lax.axis_index("tok")
    x, c = lax.div(s, 2), lax.rem(s, 2)
    z, y = lax.div(t, NY), lax.rem(t, NY)
    za, zb, zc = lax.div(z, 8), lax.div(lax.rem(z, 8), 2), lax.rem(z, 2)

    def dev_z(k):
        zp = lax.rem(z + k, NZ)
        return zp, {"seq": s, "tok": zp * NY + y}

    def dev_y(k):
        yp = lax.rem(y + k, NY)
        return yp, {"seq": s, "tok": z * NY + yp}

    def dev_s(k):
        return {"seq": lax.rem(s + k, 2 * NX), "tok": t}

    def dev_x(k):
        return {"seq": lax.rem(x + k, NX) * 2 + c, "tok": t}

    partner = {"seq": x * 2 + 1 - c, "tok": t}

    def put(src, dst, ph, dev):
        return pltpu.make_async_remote_copy(
            src_ref=src, dst_ref=dst, send_sem=ssem.at[ph], recv_sem=rsem.at[ph], device_id=dev, device_id_type=MESH
        )

    def arrived(view, ph):
        put(view, view, ph, partner).wait_recv()

    def sent(view, ph):
        put(view, view, ph, partner).wait_send()

    cache_copy = pltpu.make_async_copy(cache_ref, kv_c, lsem)
    cache_copy.start()
    az[za, zb, zc, 0:16, :] = wq_ref[...]
    az[za, zb, zc, 16:48, :] = wkv_ref[...]
    az[za, zb, zc, 48:64, :] = wo_ref[...]
    ws[s] = wq_ref[...]
    up[x, c, z] = wu_ref[...]
    down[x, c, z] = wd_ref[...]
    barrier = pltpu.get_barrier_semaphore()
    for k in range(1, 8):
        pl.semaphore_signal(barrier, inc=1, device_id=dev_s(k), device_id_type=MESH)
    for k in range(1, NY):
        pl.semaphore_signal(barrier, inc=1, device_id=dev_y(k)[1], device_id_type=MESH)

    @pl.loop(1, NZ)
    def _(k):
        pl.semaphore_signal(barrier, inc=1, device_id=dev_z(k)[1], device_id_type=MESH)

    pl.semaphore_wait(barrier, 7 + (NY - 1) + (NZ - 1))

    for k in range(1, 8):
        put(wq_ref, ws.at[s], WS, dev_s(k)).start()

    @pl.loop(1, NZ)
    def _(k):
        put(az.at[za, zb, zc], az.at[za, zb, zc], AZ, dev_z(k)[1]).start()

    arrived(ws.at[pl.ds(0, 7)], WS)
    wq_cols = jnp.concatenate([ws[i] for i in range(8)], axis=1)
    q_piece = dot_nt(wq_cols, x_ref[...]).astype(BF) * jnp.asarray(0.125, BF)
    qt[0, z, y] = q_piece

    @pl.loop(1, NZ)
    def _(k):
        put(qt.at[0, z, y], qt.at[0, z, y], 16 + GQZ, dev_z(k)[1]).start()

    @pl.loop(1, NZ)
    def _(k):
        put(wu_ref, up.at[x, c, z], UZ, dev_z(k)[1]).start()

    @pl.loop(1, NZ)
    def _(k):
        put(wd_ref, down.at[x, c, z], DZ, dev_z(k)[1]).start()

    cache_copy.wait()
    vt[:, 128:144, :] = jnp.ones((8, 16, KEYS), BF)

    @pl.loop(0, 8)
    def _(i):
        for j in range(3):
            piece = kv_c[j, :, pl.ds(pl.multiple_of(D + i * 128, 128), 128)]
            vt[i, 0:128, 128 * j : 128 * (j + 1)] = jnp.transpose(piece)

    arrived(qt.at[0, pl.ds(0, NZ - 1), 0], 16 + GQZ)
    for k in range(1, NY):
        put(qt.at[0, :, y], qt.at[0, :, y], 16 + GQY, dev_y(k)[1]).start()

    arrived(up.at[0, 0, pl.ds(0, NZ - 1)], AZ)
    for a in range(2):
        for d in range(2):
            kvw[x, c, a, d, y] = az[a, y, d, 16:48, :]
    for b in range(2):
        for d in range(2):
            ow[x, c, b, d, y] = az[lax.div(y, 2), 2 * lax.rem(y, 2) + b, d, 48:64, :]
    for k in range(1, NY):
        yp, dev = dev_y(k)
        put(az.at[:, yp, :, 16:48, :], kvw.at[x, c, :, :, y], KVY, dev).start()
        put(
            az.at[lax.div(yp, 2), pl.ds(2 * lax.rem(yp, 2), 2), :, 48:64, :], ow.at[x, c, :, :, y], OY, dev
        ).start()
    qw[x, c] = az[:, :, :, 0:16, :]
    for k in range(1, NX):
        put(qw.at[x, c], qw.at[x, c], QX, dev_x(k)).start()
    arrived(kvw.at[0, 0, :, :, pl.ds(0, 3)], KVY)
    arrived(ow.at[0, 0, :, :, pl.ds(0, 3)], OY)
    for k in range(1, NX):
        put(kvw.at[x, c], kvw.at[x, c], KVX, dev_x(k)).start()
        put(ow.at[x, c], ow.at[x, c], OX, dev_x(k)).start()

    length = len_ref[0]
    limits = [jnp.where(page_ref[0, j] >= 0, length - page_ref[0, j] * 128, 0) for j in range(3)]
    own_rows = pl.ds(pl.multiple_of(z * ROWS, ROWS), ROWS)
    current = x_ref[own_rows, :]

    for p in range(2):
        base = 16 + 9 * p
        if p == 1:
            arrived_q = jnp.concatenate([qw[i, j].reshape(256, 128) for i in range(4) for j in range(2)], axis=1)
            q_own[...] = dot_nt(current, arrived_q).astype(BF) * jnp.asarray(0.125, BF)
            qz[z] = q_own[...]

            @pl.loop(1, NZ)
            def _(k):
                put(q_own, qz.at[z], base + GQZ, dev_z(k)[1]).start()

            arrived(qz.at[pl.ds(0, NZ - 1)], base + GQZ)
            qt[1, :, y] = jnp.transpose(qz[...].reshape(TOK, 256)).reshape(NZ, 16, TOK)
            for k in range(1, NY):
                put(qt.at[1, :, y], qt.at[1, :, y], base + GQY, dev_y(k)[1]).start()
        arrived(qt.at[p, :, pl.ds(0, 3)], base + GQY)

        @pl.loop(0, NY)
        def _(j):
            g = lax.rem(y + 1 + j, NY)
            for i in range(2):
                keys = kv_c[:, :, pl.ds(pl.multiple_of(g * 256 + i * 128, 128), 128)].reshape(KEYS, 128)
                q_pair = qt[p, pl.ds(4 * g + 2 * i, 2)].reshape(2, 64, TOK)
                none = jnp.zeros((64, TOK), BF)
                both = jnp.concatenate(
                    [
                        jnp.concatenate([q_pair[0], none], axis=1),
                        jnp.concatenate([none, q_pair[1]], axis=1),
                    ],
                    axis=0,
                )
                scores = dot_nn(keys, both)
                offsets = lax.broadcasted_iota(jnp.int32, (128, 2 * TOK), 0)
                masked = jnp.concatenate(
                    [
                        jnp.where(offsets < limits[n], scores[128 * n : 128 * (n + 1)], MASKED)
                        for n in range(3)
                    ],
                    axis=0,
                )
                peaks = jnp.maximum(jnp.max(masked, axis=0, keepdims=True), FLOOR_SCORE)
                weights = jnp.exp(masked - peaks).astype(BF)
                summed = dot_nn(vt[2 * g + i], weights)
                ot[p, g, 128 * i : 128 * i + 64, :] = summed[0:64, 0:TOK].astype(BF)
                ot[p, g, 128 * i + 64 : 128 * i + 128, :] = summed[64:128, TOK : 2 * TOK].astype(BF)
                ml[p, g, 2 * i : 2 * i + 1, :] = peaks[:, 0:TOK]
                ml[p, g, 2 * i + 1 : 2 * i + 2, :] = peaks[:, TOK : 2 * TOK]
                ml[p, g, 4 + 2 * i : 5 + 2 * i, :] = summed[128:129, 0:TOK]
                ml[p, g, 5 + 2 * i : 6 + 2 * i, :] = summed[128:129, TOK : 2 * TOK]

            @pl.when(j < NY - 1)
            def _():
                dev = {"seq": s, "tok": z * NY + g}
                put(ot.at[p, g], ry.at[p, y], base + RSY, dev).start()
                put(ml.at[p, g], rym.at[p, y], base + RSYM, dev).start()

        ry[p, y] = ot[p, y]
        rym[p, y] = ml[p, y]
        if p == 0:
            arrived(qw.at[pl.ds(0, 3), 0], QX)
            arrived(kvw.at[pl.ds(0, 3), 0], KVX)
            arrived(ow.at[pl.ds(0, 3), 0], OX)
            put(kvw.at[:, c], kvw.at[:, c], KVC, partner).start()
            put(ow.at[:, c], ow.at[:, c], OC, partner).start()
            put(qw.at[:, c], qw.at[:, c], QC, partner).start()
            arrived(up.at[0, 0, pl.ds(0, NZ - 1)], UZ)
            for k in range(1, NX):
                put(up.at[x, c], up.at[x, c], UX, dev_x(k)).start()
            arrived(kvw.at[:, 0], KVC)

        w_pair = jnp.concatenate([kvw[i, j].reshape(512, 128) for i in range(4) for j in range(2)], axis=1)
        pair = dot_nt(current, w_pair)
        row_head = lax.div(lax.broadcasted_iota(jnp.int32, (64, 256), 0), 16)
        lane_head = lax.div(lax.broadcasted_iota(jnp.int32, (64, 256), 1), 64)
        own_head = row_head == lane_head
        k_block = jnp.where(own_head, jnp.concatenate([pair[:, 0:256]] * 4, axis=0), 0.0).astype(BF)
        v_block = jnp.where(own_head, jnp.concatenate([pair[:, 256:512]] * 4, axis=0), 0.0)
        q_heads = qt[p, pl.ds(4 * y, 4)].reshape(256, TOK)
        b_scores = dot_nn(k_block, q_heads).reshape(4, 16, TOK)
        b_peak = jnp.max(b_scores, axis=1)
        b_weights = jnp.exp(b_scores - b_peak[:, None, :]).astype(BF)
        b_total = jnp.sum(b_weights.astype(F32), axis=1)
        b_sum = dot_nn(jnp.transpose(v_block).astype(BF), b_weights.reshape(64, TOK))

        arrived(ry.at[p, pl.ds(0, 3)], base + RSY)
        arrived(rym.at[p, pl.ds(0, 3)], base + RSYM)
        peaks_y = rym[p, :, 0:4, :]
        peak = jnp.maximum(jnp.max(peaks_y, axis=0), b_peak)
        scale = jnp.exp(peaks_y - peak[None])
        b_scale = jnp.exp(b_peak - peak)
        total = jnp.sum(scale * rym[p, :, 4:8, :], axis=0) + b_scale * b_total
        ml2[p, 0:4, :] = peak
        ml2[p, 4:8, :] = total
        parts = []
        for h in range(4):
            rows = slice(64 * h, 64 * h + 64)
            value = b_sum[rows] * b_scale[h : h + 1]
            for i in range(NY):
                value += ry[p, i, rows, :].astype(F32) * scale[i, h : h + 1]
            parts.append(value)
        tz[p] = jnp.transpose(jnp.concatenate(parts, axis=0)).astype(BF).reshape(NZ, ROWS, 256)

        @pl.loop(1, NZ)
        def _(k):
            zp, dev = dev_z(k)
            half = pl.ds(pl.multiple_of(lax.div(zp, 8) * 128, 128), 128)
            put(tz.at[p, zp], rz.at[p, z], base + RSZ, dev).start()
            put(ml2.at[p, :, half], rzm.at[p, z], base + RSZM, dev).start()

        rz[p, z] = tz[p, z]
        rzm[p, z] = ml2[p, :, pl.ds(pl.multiple_of(za * 128, 128), 128)]
        if p == 0:
            arrived(down.at[0, 0, pl.ds(0, NZ - 1)], DZ)
            for k in range(1, NX):
                put(down.at[x, c], down.at[x, c], DX, dev_x(k)).start()
            arrived(ow.at[:, 0], OC)

        arrived(rz.at[p, pl.ds(0, NZ - 1)], base + RSZ)
        arrived(rzm.at[p, pl.ds(0, NZ - 1)], base + RSZM)
        peaks_z = rzm[p, :, 0:4, :]
        scale_z = jnp.exp(peaks_z - jnp.max(peaks_z, axis=0, keepdims=True))
        share = scale_z / jnp.sum(scale_z * rzm[p, :, 4:8, :], axis=0, keepdims=True)
        share = jnp.concatenate([share.reshape(64, 128), jnp.zeros((64, 128), F32)], axis=0)
        wt[p] = jnp.transpose(share)
        own_share = wt[p, pl.ds(pl.multiple_of(lax.rem(z, 8) * ROWS, ROWS), ROWS), :]
        lower = lax.broadcasted_iota(jnp.int32, (ROWS, 128), 1) < 64
        halves = [jnp.zeros((ROWS, 128), F32), jnp.zeros((ROWS, 128), F32)]
        for i in range(NZ):
            for n in range(2):
                low = jnp.broadcast_to(own_share[:, 4 * i + 2 * n : 4 * i + 2 * n + 1], (ROWS, 128))
                high = jnp.broadcast_to(own_share[:, 4 * i + 2 * n + 1 : 4 * i + 2 * n + 2], (ROWS, 128))
                halves[n] += jnp.where(lower, low, high) * rz[p, i, :, 128 * n : 128 * n + 128].astype(F32)
        att[p, y] = jnp.concatenate(halves, axis=1).astype(BF)
        for k in range(1, NY):
            put(att.at[p, y], att.at[p, y], base + GAY, dev_y(k)[1]).start()
        arrived(att.at[p, pl.ds(0, 3)], base + GAY)

        w_o = jnp.concatenate([ow[i, j].reshape(256, 128) for i in range(4) for j in range(2)], axis=1)
        ob[p, y] = dot_nt(jnp.concatenate([att[p, i] for i in range(NY)], axis=1), w_o)
        for k in range(1, NY):
            put(ob.at[p, y], ob.at[p, y], base + GOY, dev_y(k)[1]).start()
        if p == 0:
            arrived(up.at[pl.ds(0, 3), 0], UX)
            put(up.at[:, c], up.at[:, c], UC, partner).start()
        arrived(ob.at[p, pl.ds(0, 3)], base + GOY)
        residual = current.astype(F32) + jnp.concatenate([ob[p, i] for i in range(NY)], axis=1)
        settled = layer_norm(residual, ga_ref[...]).astype(BF)

        if p == 0:
            arrived(up.at[:, 0], UC)
        w_u = jnp.concatenate([up[i, j].reshape(D, 128) for i in range(4) for j in range(2)], axis=1)
        product = dot_nt(settled, w_u)
        hidden = (0.5 * product * (1.0 + lax.erf(product * (0.5**0.5)))).astype(BF)
        if p == 0:
            arrived(down.at[pl.ds(0, 3), 0], DX)
            put(down.at[:, c], down.at[:, c], DC, partner).start()
            arrived(down.at[:, 0], DC)
        w_d = jnp.concatenate([down[i, j].reshape(D, 128) for i in range(4) for j in range(2)], axis=1)
        fp[p, y] = dot_nn(hidden, w_d).astype(BF)
        for k in range(1, NY):
            put(fp.at[p, y], fp.at[p, y], base + RFY, dev_y(k)[1]).start()
        if p == 0:
            arrived(qw.at[:, 0], QC)
        arrived(fp.at[p, pl.ds(0, 3)], base + RFY)
        projected = fp[p, 0].astype(F32) + fp[p, 1].astype(F32) + fp[p, 2].astype(F32) + fp[p, 3].astype(F32)
        finished = layer_norm(settled.astype(F32) + projected, gm_ref[...])
        taken = accept_ref[p, :, 0:1] == 1
        current = jnp.where(taken, finished, current.astype(F32)).astype(BF)

    fin[...] = current
    quarter = pl.ds(pl.multiple_of(y * 256, 256), 256)
    fz[z] = fin[:, quarter]

    @pl.loop(1, NZ)
    def _(k):
        put(fz.at[z], fz.at[z], FIN_Z, dev_z(k)[1]).start()

    arrived(fz.at[pl.ds(0, NZ - 1)], FIN_Z)
    for k in range(1, NY):
        put(fz, out_ref.at[:, :, quarter], FIN_Y, dev_y(k)[1]).start()
    out_ref[:, :, quarter] = fz[...]
    arrived(out_ref.at[:, :, pl.ds(0, 768)], FIN_Y)

    sent(ws.at[pl.ds(0, 7)], WS)
    sent(up.at[0, 0, pl.ds(0, NZ - 1)], AZ)
    sent(kvw.at[0, 0, :, :, pl.ds(0, 3)], KVY)
    sent(ow.at[0, 0, :, :, pl.ds(0, 3)], OY)
    for ref, xs, cs in ((qw, QX, QC), (kvw, KVX, KVC), (ow, OX, OC), (up, UX, UC), (down, DX, DC)):
        sent(ref.at[pl.ds(0, 3), 0], xs)
        sent(ref.at[:, 0], cs)
    sent(up.at[0, 0, pl.ds(0, NZ - 1)], UZ)
    sent(down.at[0, 0, pl.ds(0, NZ - 1)], DZ)
    for p in range(2):
        base = 16 + 9 * p
        sent(qt.at[p, pl.ds(0, NZ - 1), 0], base + GQZ)
        sent(qt.at[p, :, pl.ds(0, 3)], base + GQY)
        sent(ry.at[p, pl.ds(0, 3)], base + RSY)
        sent(rym.at[p, pl.ds(0, 3)], base + RSYM)
        sent(rz.at[p, pl.ds(0, NZ - 1)], base + RSZ)
        sent(rzm.at[p, pl.ds(0, NZ - 1)], base + RSZM)
        sent(att.at[p, pl.ds(0, 3)], base + GAY)
        sent(ob.at[p, pl.ds(0, 3)], base + GOY)
        sent(fp.at[p, pl.ds(0, 3)], base + RFY)
    sent(fz.at[pl.ds(0, NZ - 1)], FIN_Z)
    sent(out_ref.at[:, :, pl.ds(0, 768)], FIN_Y)


def shards(
    block_in, accept, cache_len, slot_page, cache_kv, w_query, w_key_value, w_out, gain_attn, w_up, w_down, gain_mlp
):
    z = lax.div(lax.axis_index("tok"), NY)
    taken = lax.dynamic_slice_in_dim(accept[:, 0], z * ROWS, ROWS, 1)
    taken = jnp.broadcast_to(taken[:, :, None], (2, ROWS, 128))
    vmem = pl.BlockSpec(memory_space=pltpu.VMEM)
    smem = pl.BlockSpec(memory_space=pltpu.SMEM)
    result = pl.pallas_call(
        kernel,
        out_shape=jax.ShapeDtypeStruct((NZ, ROWS, D), BF),
        in_specs=[vmem, vmem, smem, smem, pl.BlockSpec(memory_space=pl.ANY)] + [vmem] * 7,
        out_specs=vmem,
        scratch_shapes=[
            pltpu.VMEM((3, 128, 2 * D), BF),
            pltpu.VMEM((8, 144, KEYS), BF),
            pltpu.VMEM((8, 16, 128), BF),
            pltpu.VMEM((2, 4, 2, 64, 128), BF),
            pltpu.VMEM((4, 2, 2, 4, 2, 16, 128), BF),
            pltpu.VMEM((4, 2, 2, 2, 4, 32, 128), BF),
            pltpu.VMEM((4, 2, 2, 2, 4, 16, 128), BF),
            pltpu.VMEM((4, 2, NZ, 64, 128), BF),
            pltpu.VMEM((4, 2, NZ, 64, 128), BF),
            pltpu.VMEM((ROWS, 256), BF),
            pltpu.VMEM((NZ, ROWS, 256), BF),
            pltpu.VMEM((2, NZ, NY, 16, TOK), BF),
            pltpu.VMEM((2, NY, 256, TOK), BF),
            pltpu.VMEM((2, NY, 8, TOK), F32),
            pltpu.VMEM((2, NY, 256, TOK), BF),
            pltpu.VMEM((2, NY, 8, TOK), F32),
            pltpu.VMEM((2, NZ, ROWS, 256), BF),
            pltpu.VMEM((2, 8, TOK), F32),
            pltpu.VMEM((2, NZ, ROWS, 256), BF),
            pltpu.VMEM((2, NZ, 8, 128), F32),
            pltpu.VMEM((2, 128, 128), F32),
            pltpu.VMEM((2, NY, ROWS, 256), BF),
            pltpu.VMEM((2, NY, ROWS, 256), F32),
            pltpu.VMEM((2, NY, ROWS, D), BF),
            pltpu.VMEM((ROWS, D), BF),
            pltpu.VMEM((NZ, ROWS, 256), BF),
            pltpu.SemaphoreType.DMA((N_SEM,)),
            pltpu.SemaphoreType.DMA((N_SEM,)),
            pltpu.SemaphoreType.DMA,
        ],
        compiler_params=pltpu.CompilerParams(
            collective_id=0, has_side_effects=True, vmem_limit_bytes=48 * 1024 * 1024
        ),
    )(
        block_in[0],
        taken,
        cache_len,
        slot_page,
        cache_kv[0],
        w_query.T,
        w_key_value.T,
        w_out.T,
        w_up.T,
        w_down,
        gain_attn[None],
        gain_mlp[None],
    )
    return result.reshape(1, TOK, D)


def solution(mesh):
    in_specs = (
        P("seq", None, None),
        P(None, "seq", None),
        P("seq"),
        P("seq", "tok"),
        P("seq", "tok", None, None),
        P("seq", "tok"),
        P("seq", "tok"),
        P("seq", "tok"),
        P(),
        P("seq", "tok"),
        P("tok", "seq"),
        P(),
    )
    out_specs = P("seq", None, None)
    return jax.shard_map(shards, mesh=mesh, in_specs=in_specs, out_specs=out_specs, check_vma=False)
```

```python
import jax
import jax.numpy as jnp
from jax import lax
from jax.experimental import pallas as pl
from jax.experimental.pallas import tpu as pltpu
from jax.sharding import PartitionSpec as P

MESH = pl.DeviceIdType.MESH
BF = jnp.bfloat16
F32 = jnp.float32

D = 1024
TOK = 256
NZ, NY, NX = 16, 4, 4
ROWS = TOK // NZ
KEYS = 384
EPSILON = 1e-05
FLOOR_SCORE = -1e30
MASKED = -3e38

(WS, KVZ, OZ, QZ, KVX, OX, QX, KVC, OC, QC, UX, DX, UC, DC, LIM) = range(15)
CY = 15
UP, DOWN = 19, 23
PASS = 27
(GQZ, RSZ, RSZM, GAY, GOY, RFY) = range(6)
FIN_Y, FIN_Z = PASS + 12, PASS + 12
N_SEM = PASS + 28


def dot_nn(a, b):
    return lax.dot_general(a, b, (((1,), (0,)), ((), ())), preferred_element_type=F32)


def dot_nt(a, b):
    return lax.dot_general(a, b, (((1,), (1,)), ((), ())), preferred_element_type=F32)


def layer_norm(values, gain):
    average = jnp.mean(values, axis=-1, keepdims=True)
    centered = values - average
    variance = jnp.mean(centered * centered, axis=-1, keepdims=True)
    return centered * lax.rsqrt(variance + EPSILON) * gain


def kernel(
    len_ref, page_ref, x_hbm, accept_hbm, cache_ref, wq_ref, wkv_ref, wo_ref, wu_ref, wd_ref, ga_hbm, gm_hbm,
    out_ref,
    x_ref, accept_ref, ga_ref, gm_ref, kvb, vt, lim, ws, qw, kvw, ow, up, down,
    hold, qz, qt, po, pm, tz, tzm, rz, rzm, att, ob, fp, fin, fz,
    ssem, rsem, lsem,
):
    s, t = lax.axis_index("seq"), lax.axis_index("tok")
    x, c = lax.div(s, 2), lax.rem(s, 2)
    z, y = lax.div(t, NY), lax.rem(t, NY)
    za, zc = lax.div(z, 8), lax.rem(z, 2)
    to_kv = lax.div(lax.rem(z, 8), 2)
    to_q = lax.div(z, 4)
    to_t = lax.rem(t, NZ) * NY + lax.div(t, NZ)
    from_t = (NY * y + lax.div(z, NY)) * NY + lax.rem(z, NY)

    def dev_z(k, row=None):
        zp = lax.rem(z + k, NZ)
        return zp, {"seq": s, "tok": zp * NY + (y if row is None else row)}

    def dev_y(k):
        yp = lax.rem(y + k, NY)
        return yp, {"seq": s, "tok": z * NY + yp}

    def dev_s(k, tok):
        return {"seq": lax.rem(s + k, 2 * NX), "tok": tok}

    def dev_x(k):
        return {"seq": lax.rem(x + k, NX) * 2 + c, "tok": t}

    partner = {"seq": x * 2 + 1 - c, "tok": t}

    def put(src, dst, ph, dev, rph=None):
        return pltpu.make_async_remote_copy(
            src_ref=src,
            dst_ref=dst,
            send_sem=ssem.at[ph],
            recv_sem=rsem.at[ph if rph is None else rph],
            device_id=dev,
            device_id_type=MESH,
        )

    def arrived(view, ph):
        put(view, view, ph, partner).wait_recv()

    def sent(view, ph):
        put(view, view, ph, partner).wait_send()

    def here(src, dst, ph):
        pltpu.make_async_copy(src, dst, rsem.at[ph]).start()

    def tell(dev):
        pl.semaphore_signal(barrier, inc=1, device_id=dev, device_id_type=MESH)

    def lanes(start, size):
        return pl.ds(pl.multiple_of(start, size), size)

    local = [
        pltpu.make_async_copy(a, b, lsem.at[i])
        for i, (a, b) in enumerate(
            (
                (x_hbm, x_ref),
                (cache_ref.at[:, :, lanes(y * 256, 256)], kvb.at[y, 0]),
                (cache_ref.at[:, :, lanes(D + y * 256, 256)], kvb.at[y, 1]),
                (wu_ref, up.at[x, c, z]),
                (wd_ref, down.at[x, c, z]),
                (accept_hbm, accept_ref),
                (ga_hbm, ga_ref),
                (gm_hbm, gm_ref),
            )
        )
    ]
    for copy in local:
        copy.start()

    barrier = pltpu.get_barrier_semaphore()
    for k in range(8):
        @pl.when((k > 0) | (from_t != t))
        def _():
            tell(dev_s(k, from_t))
    for k in range(1, NX):
        tell(dev_x(k))
    tell(partner)
    for k in range(1, NY):
        tell(dev_y(k)[1])

    @pl.loop(1, NZ)
    def _(k):
        tell(dev_z(k)[1])

    @pl.loop(0, NZ)
    def _(i):
        zs, ys = 8 * lax.div(i, 8) + 2 * y + lax.rem(lax.div(i, 4), 2), lax.rem(i, 4)

        @pl.when((zs != z) | (ys != y))
        def _():
            tell({"seq": s, "tok": zs * NY + ys})

    @pl.loop(0, NZ)
    def _(i):
        zs, ys = 4 * y + lax.div(i, 4), lax.rem(i, 4)

        @pl.when((zs != z) | (ys != y))
        def _():
            tell({"seq": s, "tok": zs * NY + ys})

    others = (to_t != t).astype(jnp.int32) + (to_kv != y).astype(jnp.int32) + (to_q != y).astype(jnp.int32)
    pl.semaphore_wait(barrier, 7 + NX + (NY - 1) + 3 * (NZ - 1) + others)

    for k in range(8):
        @pl.when((k > 0) | (to_t != t))
        def _():
            put(wq_ref, ws.at[s], WS, dev_s(k, to_t)).start()

    @pl.when(to_t == t)
    def _():
        here(wq_ref, ws.at[s], WS)

    for k in (1, 3, 2):
        yp, dev = dev_y(k)
        put(cache_ref.at[:, :, lanes(yp * 256, 256)], kvb.at[y, 0], CY + k, dev).start()
        put(cache_ref.at[:, :, lanes(D + yp * 256, 256)], kvb.at[y, 1], CY + k, dev).start()
    length = len_ref[0].astype(F32)
    slot_row = lax.broadcasted_iota(jnp.int32, (8, 128), 0)
    limits = jnp.zeros((8, 128), F32)
    for j in range(3):
        page = page_ref[0, j].astype(F32)
        limits = jnp.where(slot_row == j, jnp.where(page >= 0, length - page * 128, 0.0), limits)
    lim[y] = limits
    for k in range(1, NY):
        put(lim.at[y], lim.at[y], LIM, dev_y(k)[1]).start()

    def spread(src, dst, ph, row):
        @pl.loop(1, NZ)
        def _(k):
            put(src, dst, ph, dev_z(k, row)[1]).start()

        @pl.when(row != y)
        def _():
            put(src, dst, ph, dev_z(0, row)[1]).start()

        @pl.when(row == y)
        def _():
            here(src, dst, ph)

    spread(wkv_ref, kvw.at[x, c, za, zc, y], KVZ, to_kv)
    arrived(ws, WS)
    local[0].wait()
    wq_cols = jnp.concatenate([ws[i] for i in range(8)], axis=1)
    qt[0, z] = dot_nt(wq_cols, x_ref[...]).astype(BF) * jnp.asarray(0.125, BF)

    @pl.loop(1, NZ)
    def _(k):
        put(qt.at[0, z], qt.at[0, z], PASS + GQZ, dev_z(k)[1]).start()

    def direct(ref, ph):
        for k in (4, 12):
            put(ref.at[x, c, z], ref.at[x, c, z], ph, dev_z(k)[1], ph + (1 if k == 4 else 2)).start()
        for k in (1, 15, 2, 14, 3, 13):
            put(ref.at[x, c, z], ref.at[x, c, z], ph, dev_z(k)[1]).start()

    def relay(ref, ph):
        left, right = lax.rem(z + 12, NZ), lax.rem(z + 4, NZ)
        arrived(ref.at[x, c, left], ph + 1)
        for k in (4, 3, 2, 1):
            put(ref.at[x, c, left], ref.at[x, c, left], ph + 3, dev_z(k)[1]).start()
        arrived(ref.at[x, c, right], ph + 2)
        for k in (13, 14, 15):
            put(ref.at[x, c, right], ref.at[x, c, right], ph + 3, dev_z(k)[1]).start()

    def to_x(ref, ph):
        for k in (1, 3, 2):
            put(ref.at[x, c], ref.at[x, c], ph, dev_x(k)).start()

    def to_core(ref, xs, cs):
        arrived(ref.at[pl.ds(0, 3), 0], xs)
        put(ref.at[:, c], ref.at[:, c], cs, partner).start()

    def over_z(ref, ph, xs):
        arrived(ref.at[0, 0, pl.ds(0, 6)], ph)
        arrived(ref.at[0, 0, pl.ds(0, 7)], ph + 3)
        to_x(ref, xs)

    spread(wo_ref, ow.at[x, c, lax.rem(z, 4), y], OZ, to_q)
    local[3].wait()
    direct(up, UP)
    local[4].wait()
    direct(down, DOWN)
    spread(wq_ref, qw.at[x, c, lax.rem(z, 4), y], QZ, to_q)

    vt[:, :, 128:144, :] = jnp.ones((NY, 2, 16, KEYS), BF)

    def turn(j):
        for i in range(2):
            for n in range(3):
                vt[j, i, 0:128, 128 * n : 128 * (n + 1)] = jnp.transpose(kvb[j, 1, n, :, 128 * i : 128 * i + 128])

    local[1].wait()
    local[2].wait()
    turn(y)
    arrived(kvw.at[0, 0], KVZ)
    to_x(kvw, KVX)
    for k in (1, 3, 2):
        src = lax.rem(y + NY - k, NY)
        arrived(kvb.at[src], CY + k)
        turn(src)
    arrived(lim.at[pl.ds(0, 3)], LIM)
    for i in range(5, 8):
        local[i].wait()

    own_rows = pl.ds(pl.multiple_of(z * ROWS, ROWS), ROWS)
    current = x_ref[own_rows, :]

    for p in range(2):
        base = PASS + 6 * p
        if p == 1:
            w_q = jnp.concatenate([qw[i, j].reshape(256, 128) for i in range(4) for j in range(2)], axis=1)
            qz[z] = dot_nt(current, w_q).astype(BF) * jnp.asarray(0.125, BF)

            @pl.loop(1, NZ)
            def _(k):
                put(qz.at[z], qz.at[z], base + GQZ, dev_z(k)[1]).start()

            arrived(qz.at[pl.ds(0, NZ - 1)], base + GQZ)
            qt[1] = jnp.transpose(qz[...].reshape(TOK, 256)).reshape(NZ, 16, TOK)
        else:
            arrived(qt.at[p, pl.ds(0, NZ - 1)], base + GQZ)

        @pl.loop(0, NY)
        def _(j):
            if p == 0:
                @pl.when(j == 1)
                def _():
                    arrived(ow.at[0, 0], OZ)
                    to_x(ow, OX)
                    to_core(kvw, KVX, KVC)

                @pl.when(j == 2)
                def _():
                    relay(up, UP)

                @pl.when(j == 3)
                def _():
                    relay(down, DOWN)

            for i in range(2):
                keys = kvb[j, 0, :, :, 128 * i : 128 * i + 128].reshape(KEYS, 128)
                q_pair = qt[p, 8 * i : 8 * i + 8].reshape(2, 64, TOK)
                none = jnp.zeros((64, TOK), BF)
                both = jnp.concatenate(
                    [
                        jnp.concatenate([q_pair[0], none], axis=1),
                        jnp.concatenate([none, q_pair[1]], axis=1),
                    ],
                    axis=0,
                )
                scores = dot_nn(keys, both)
                offsets = lax.broadcasted_iota(jnp.int32, (128, 2 * TOK), 0).astype(F32)
                masked = jnp.concatenate(
                    [
                        jnp.where(
                            offsets < jnp.concatenate([lim[j, n : n + 1, :]] * 4, axis=1),
                            scores[128 * n : 128 * (n + 1)],
                            MASKED,
                        )
                        for n in range(3)
                    ],
                    axis=0,
                )
                peaks = jnp.maximum(jnp.max(masked, axis=0, keepdims=True), FLOOR_SCORE)
                weights = jnp.exp(masked - peaks).astype(BF)
                summed = dot_nn(vt[j, i], weights)
                po[j, 128 * i : 128 * i + 64, :] = summed[0:64, 0:TOK]
                po[j, 128 * i + 64 : 128 * i + 128, :] = summed[64:128, TOK : 2 * TOK]
                pm[j, 2 * i : 2 * i + 1, :] = peaks[:, 0:TOK]
                pm[j, 2 * i + 1 : 2 * i + 2, :] = peaks[:, TOK : 2 * TOK]
                pm[j, 4 + 2 * i : 5 + 2 * i, :] = summed[128:129, 0:TOK]
                pm[j, 5 + 2 * i : 6 + 2 * i, :] = summed[128:129, TOK : 2 * TOK]

        if p == 0:
            over_z(up, UP, UX)
            arrived(kvw.at[:, 0], KVC)

        w_pair = jnp.concatenate([kvw[i, j].reshape(512, 128) for i in range(4) for j in range(2)], axis=1)
        pair = dot_nt(current, w_pair)
        row_head = lax.div(lax.broadcasted_iota(jnp.int32, (64, 256), 0), 16)
        lane_head = lax.div(lax.broadcasted_iota(jnp.int32, (64, 256), 1), 64)
        own_head = row_head == lane_head
        k_block = jnp.where(own_head, jnp.concatenate([pair[:, 0:256]] * 4, axis=0), 0.0).astype(BF)
        v_block = jnp.where(own_head, jnp.concatenate([pair[:, 256:512]] * 4, axis=0), 0.0)
        b_scores = dot_nn(k_block, qt[p].reshape(256, TOK)).reshape(4, 16, TOK)
        b_peak = jnp.max(b_scores, axis=1)
        b_weights = jnp.exp(b_scores - b_peak[:, None, :]).astype(BF)
        b_total = jnp.sum(b_weights.astype(F32), axis=1)
        b_sum = dot_nn(jnp.transpose(v_block).astype(BF), b_weights.reshape(64, TOK))

        peaks_y = pm[:, 0:4, :]
        peak = jnp.maximum(jnp.max(peaks_y, axis=0), b_peak)
        scale = jnp.exp(peaks_y - peak[None])
        b_scale = jnp.exp(b_peak - peak)
        total = jnp.sum(scale * pm[:, 4:8, :], axis=0) + b_scale * b_total
        parts = []
        for h in range(4):
            rows = slice(64 * h, 64 * h + 64)
            value = b_sum[rows] * b_scale[h : h + 1]
            for i in range(NY):
                value += po[i, rows, :] * scale[i, h : h + 1]
            parts.append(value)
        tz[p] = jnp.transpose(jnp.concatenate(parts, axis=0)).astype(BF).reshape(NZ, ROWS, 256)
        both = jnp.concatenate([peak, total], axis=0)
        belongs = lax.broadcasted_iota(jnp.int32, (8, 128), 0) == lax.div(
            lax.broadcasted_iota(jnp.int32, (8, 128), 1), ROWS
        )
        steps = [pltpu.roll(both[:, 128 * i : 128 * i + 128], 0, 1, stride=ROWS, stride_axis=0) for i in range(2)]
        for i in range(NZ):
            moved = pltpu.roll(steps[i // 8], (128 - ROWS * (i % 8)) % 128, 1)
            tzm[p, i] = jnp.sum(jnp.where(belongs, moved, 0.0), axis=0, keepdims=True)

        @pl.loop(1, NZ)
        def _(k):
            zp, dev = dev_z(k)
            put(tzm.at[p, zp], rzm.at[p, z], base + RSZM, dev).start()
            put(tz.at[p, zp], rz.at[p, z], base + RSZ, dev).start()

        rz[p, z] = tz[p, z]
        rzm[p, z] = tzm[p, z]
        if p == 0:
            over_z(down, DOWN, DX)
            to_core(ow, OX, OC)

        arrived(rzm.at[p, pl.ds(0, NZ - 1)], base + RSZM)
        stats = rzm[p].reshape(NZ, 128)
        scale_z = jnp.exp(stats - jnp.max(stats, axis=0, keepdims=True))
        share = scale_z / jnp.sum(scale_z * pltpu.roll(stats, 64, 1), axis=0, keepdims=True)
        share = jnp.transpose(jnp.concatenate([share, jnp.zeros((128 - NZ, 128), F32)], axis=0))
        arrived(rz.at[p, pl.ds(0, NZ - 1)], base + RSZ)
        lower = lax.broadcasted_iota(jnp.int32, (ROWS, 128), 1) < 64
        halves = [jnp.zeros((ROWS, 128), F32), jnp.zeros((ROWS, 128), F32)]
        for i in range(NZ):
            for n in range(2):
                low = jnp.broadcast_to(share[32 * n : 32 * n + 16, i : i + 1], (ROWS, 128))
                high = jnp.broadcast_to(share[32 * n + 16 : 32 * n + 32, i : i + 1], (ROWS, 128))
                halves[n] += jnp.where(lower, low, high) * rz[p, i, :, 128 * n : 128 * n + 128].astype(F32)
        att[p, y] = jnp.concatenate(halves, axis=1).astype(BF)
        for k in range(1, NY):
            put(att.at[p, y], att.at[p, y], base + GAY, dev_y(k)[1]).start()
        if p == 0:
            arrived(ow.at[:, 0], OC)
            arrived(qw.at[0, 0], QZ)
            to_x(qw, QX)
        arrived(att.at[p, pl.ds(0, 3)], base + GAY)

        w_o = jnp.concatenate([ow[i, j].reshape(256, 128) for i in range(4) for j in range(2)], axis=1)
        ob[p, y] = dot_nt(jnp.concatenate([att[p, i] for i in range(NY)], axis=1), w_o)
        for k in range(1, NY):
            put(ob.at[p, y], ob.at[p, y], base + GOY, dev_y(k)[1]).start()
        if p == 0:
            to_core(up, UX, UC)
        arrived(ob.at[p, pl.ds(0, 3)], base + GOY)
        residual = current.astype(F32) + jnp.concatenate([ob[p, i] for i in range(NY)], axis=1)
        settled = layer_norm(residual, ga_ref[...]).astype(BF)

        if p == 0:
            arrived(up.at[:, 0], UC)
        w_u = jnp.concatenate([up[i, j].reshape(D, 128) for i in range(4) for j in range(2)], axis=1)
        product = dot_nt(settled, w_u)
        hidden = (0.5 * product * (1.0 + lax.erf(product * (0.5**0.5)))).astype(BF)
        if p == 0:
            to_core(down, DX, DC)
            arrived(down.at[:, 0], DC)
        w_d = jnp.concatenate([down[i, j].reshape(D, 128) for i in range(4) for j in range(2)], axis=1)
        fp[p, y] = dot_nn(hidden, w_d).astype(BF)
        for k in range(1, NY):
            put(fp.at[p, y], fp.at[p, y], base + RFY, dev_y(k)[1]).start()
        if p == 0:
            to_core(qw, QX, QC)
            arrived(qw.at[:, 0], QC)
        arrived(fp.at[p, pl.ds(0, 3)], base + RFY)
        projected = fp[p, 0].astype(F32) + fp[p, 1].astype(F32) + fp[p, 2].astype(F32) + fp[p, 3].astype(F32)
        finished = layer_norm(settled.astype(F32) + projected, gm_ref[...])
        own_token = lax.broadcasted_iota(jnp.int32, (ROWS, TOK), 1) == z * ROWS + lax.broadcasted_iota(
            jnp.int32, (ROWS, TOK), 0
        )
        taken = jnp.sum(jnp.where(own_token, accept_ref[p].astype(F32), 0.0), axis=1, keepdims=True) > 0.5
        current = jnp.where(taken, finished, current.astype(F32)).astype(BF)

    fin[...] = current
    quarter = lanes(y * 256, 256)
    fz[z] = fin[:, quarter]

    def hand_on(zp):
        for k in range(1, NY):
            put(fz.at[zp], out_ref.at[zp, :, quarter], FIN_Y, dev_y(k)[1]).start()

    def in_turn(i):
        near = lax.div(i, 2) + 1
        return jnp.where(lax.rem(i, 2) == 0, near, NZ - near)

    @pl.loop(0, NZ - 1)
    def _(i):
        k = in_turn(i)
        put(fz.at[z], fz.at[z], FIN_Z + k, dev_z(k)[1]).start()

    hand_on(z)

    @pl.loop(0, NZ - 1)
    def _(i):
        k = in_turn(i)
        zp = lax.rem(z + NZ - k, NZ)
        arrived(fz.at[zp], FIN_Z + k)
        hand_on(zp)

    out_ref[:, :, quarter] = fz[...]
    arrived(out_ref.at[:, :, pl.ds(0, 768)], FIN_Y)

    def sent_but_own(ref, axis_end, ph, own):
        @pl.when(own)
        def _():
            sent(ref.at[pl.ds(0, axis_end - 1)], ph)

        @pl.when(jnp.logical_not(own))
        def _():
            sent(ref.at[pl.ds(0, axis_end)], ph)

    sent_but_own(ws, 8, WS, to_t == t)
    sent_but_own(qz, NZ, KVZ, to_kv == y)
    sent_but_own(hold, NZ, OZ, to_q == y)
    sent_but_own(hold, NZ, QZ, to_q == y)
    for ref, xs, cs in ((qw, QX, QC), (kvw, KVX, KVC), (ow, OX, OC), (up, UX, UC), (down, DX, DC)):
        sent(ref.at[pl.ds(0, 3), 0], xs)
        sent(ref.at[:, 0], cs)
    for ph in (UP, DOWN):
        sent(up.at[0, 0, pl.ds(0, 8)], ph)
        sent(up.at[0, 0, pl.ds(0, 7)], ph + 3)
    for k in range(1, NY):
        sent(kvb.at[0], CY + k)
    sent(lim.at[pl.ds(0, 3)], LIM)
    for p in range(2):
        base = PASS + 6 * p
        sent(qz.at[pl.ds(0, NZ - 1)], base + GQZ)
        sent(rz.at[p, pl.ds(0, NZ - 1)], base + RSZ)
        sent(rzm.at[p, pl.ds(0, NZ - 1)], base + RSZM)
        sent(att.at[p, pl.ds(0, 3)], base + GAY)
        sent(ob.at[p, pl.ds(0, 3)], base + GOY)
        sent(fp.at[p, pl.ds(0, 3)], base + RFY)

    @pl.loop(1, NZ)
    def _(k):
        sent(fz.at[0], FIN_Z + k)

    sent(out_ref.at[:, :, pl.ds(0, 768)], FIN_Y)


def shards(
    block_in, accept, cache_len, slot_page, cache_kv, w_query, w_key_value, w_out, gain_attn, w_up, w_down, gain_mlp
):
    smem = pl.BlockSpec(memory_space=pltpu.SMEM)
    result = pl.pallas_call(
        kernel,
        out_shape=jax.ShapeDtypeStruct((NZ, ROWS, D), BF),
        in_specs=[smem, smem] + [pl.BlockSpec(memory_space=pl.ANY)] * 10,
        out_specs=pl.BlockSpec(memory_space=pltpu.VMEM),
        scratch_shapes=[
            pltpu.VMEM((TOK, D), BF),
            pltpu.VMEM((2, 1, TOK), jnp.int32),
            pltpu.VMEM((1, D), F32),
            pltpu.VMEM((1, D), F32),
            pltpu.VMEM((NY, 2, 3, 128, 256), BF),
            pltpu.VMEM((NY, 2, 144, KEYS), BF),
            pltpu.VMEM((NY, 8, 128), F32),
            pltpu.VMEM((8, 16, 128), BF),
            pltpu.VMEM((4, 2, 4, 4, 16, 128), BF),
            pltpu.VMEM((4, 2, 2, 2, 4, 32, 128), BF),
            pltpu.VMEM((4, 2, 4, 4, 16, 128), BF),
            pltpu.VMEM((4, 2, NZ, 64, 128), BF),
            pltpu.VMEM((4, 2, NZ, 64, 128), BF),
            pltpu.VMEM((NZ, 16, 128), BF),
            pltpu.VMEM((NZ, ROWS, 256), BF),
            pltpu.VMEM((2, NZ, 16, TOK), BF),
            pltpu.VMEM((NY, 256, TOK), F32),
            pltpu.VMEM((NY, 8, TOK), F32),
            pltpu.VMEM((2, NZ, ROWS, 256), BF),
            pltpu.VMEM((2, NZ, 1, 128), F32),
            pltpu.VMEM((2, NZ, ROWS, 256), BF),
            pltpu.VMEM((2, NZ, 1, 128), F32),
            pltpu.VMEM((2, NY, ROWS, 256), BF),
            pltpu.VMEM((2, NY, ROWS, 256), F32),
            pltpu.VMEM((2, NY, ROWS, D), BF),
            pltpu.VMEM((ROWS, D), BF),
            pltpu.VMEM((NZ, ROWS, 256), BF),
            pltpu.SemaphoreType.DMA((N_SEM,)),
            pltpu.SemaphoreType.DMA((N_SEM,)),
            pltpu.SemaphoreType.DMA((8,)),
        ],
        compiler_params=pltpu.CompilerParams(
            collective_id=0, has_side_effects=True, vmem_limit_bytes=48 * 1024 * 1024
        ),
    )(
        cache_len,
        slot_page,
        block_in[0],
        accept,
        cache_kv[0],
        w_query.T,
        w_key_value.T,
        w_out.T,
        w_up.T,
        w_down,
        gain_attn[None],
        gain_mlp[None],
    )
    return result.reshape(1, TOK, D)


def solution(mesh):
    in_specs = (
        P("seq", None, None),
        P(None, "seq", None),
        P("seq"),
        P("seq", "tok"),
        P("seq", "tok", None, None),
        P("seq", "tok"),
        P("seq", "tok"),
        P("seq", "tok"),
        P(),
        P("seq", "tok"),
        P("tok", "seq"),
        P(),
    )
    out_specs = P("seq", None, None)
    return jax.shard_map(shards, mesh=mesh, in_specs=in_specs, out_specs=out_specs, check_vma=False)
```

```python
import jax
import jax.numpy as jnp
from jax import lax
from jax.experimental import pallas as pl
from jax.experimental.pallas import tpu as pltpu
from jax.sharding import PartitionSpec as P

MESH = pl.DeviceIdType.MESH
BF = jnp.bfloat16
F32 = jnp.float32

D = 1024
TOK = 256
NZ, NY, NX = 16, 4, 4
ROWS = TOK // NZ
KEYS = 384
EPSILON = 1e-05
FLOOR_SCORE = -1e30
MASKED = -3e38

(WS, KVZ, OZ, QZ, KVX, OX, QX, KVC, OC, QC, WS2, KPZ, LIM) = range(13)
CY = 13
UP, DOWN = 17, 25
PASS = 33
FAR_FIRST = (8, 7, 9, 6, 10, 5, 11, 4, 12, 3, 13, 2, 14, 1, 15)
(GQZ, RSZ, RSZM, GAY, GOY, RFY) = range(6)
FIN_Y, FIN_Z = PASS + 12, PASS + 12
N_SEM = PASS + 28


def dot_nn(a, b):
    return lax.dot_general(a, b, (((1,), (0,)), ((), ())), preferred_element_type=F32)


def dot_nt(a, b):
    return lax.dot_general(a, b, (((1,), (1,)), ((), ())), preferred_element_type=F32)


def layer_norm(values, gain):
    average = jnp.mean(values, axis=-1, keepdims=True)
    centered = values - average
    variance = jnp.mean(centered * centered, axis=-1, keepdims=True)
    return centered * lax.rsqrt(variance + EPSILON) * gain


def kernel(
    len_ref, page_ref, x_hbm, accept_hbm, cache_ref, wq_ref, wkv_ref, wo_ref, wu_ref, wd_ref, ga_hbm, gm_hbm,
    out_ref,
    x_ref, accept_ref, ga_ref, gm_ref, kvb, vt, lim, ws, ws2, kp, rkp, qw, kvw, ow, up, down,
    hold, qz, qt, po, pm, tz, tzm, rz, rzm, att, ob, fp, fin, fz,
    ssem, rsem, lsem,
):
    s, t = lax.axis_index("seq"), lax.axis_index("tok")
    x, c = lax.div(s, 2), lax.rem(s, 2)
    z, y = lax.div(t, NY), lax.rem(t, NY)
    za, zc = lax.div(z, 8), lax.rem(z, 2)
    to_kv = lax.div(lax.rem(z, 8), 2)
    to_q = lax.div(z, 4)
    to_t = lax.rem(t, NZ) * NY + lax.div(t, NZ)
    from_t = (NY * y + lax.div(z, NY)) * NY + lax.rem(z, NY)
    to_p = (lax.rem(t, 8) + 8 * lax.div(t, 32)) * NY + lax.rem(lax.div(t, 8), 4)
    from_p = 8 * y + z + 24 * za

    def dev_z(k, row=None):
        zp = lax.rem(z + k, NZ)
        return zp, {"seq": s, "tok": zp * NY + (y if row is None else row)}

    def dev_y(k):
        yp = lax.rem(y + k, NY)
        return yp, {"seq": s, "tok": z * NY + yp}

    def dev_s(k, tok):
        return {"seq": lax.rem(s + k, 2 * NX), "tok": tok}

    def dev_x(k):
        return {"seq": lax.rem(x + k, NX) * 2 + c, "tok": t}

    partner = {"seq": x * 2 + 1 - c, "tok": t}

    def put(src, dst, ph, dev, rph=None):
        return pltpu.make_async_remote_copy(
            src_ref=src,
            dst_ref=dst,
            send_sem=ssem.at[ph],
            recv_sem=rsem.at[ph if rph is None else rph],
            device_id=dev,
            device_id_type=MESH,
        )

    def arrived(view, ph):
        put(view, view, ph, partner).wait_recv()

    def sent(view, ph):
        put(view, view, ph, partner).wait_send()

    def here(src, dst, ph):
        pltpu.make_async_copy(src, dst, rsem.at[ph]).start()

    def tell(dev):
        pl.semaphore_signal(barrier, inc=1, device_id=dev, device_id_type=MESH)

    def lanes(start, size):
        return pl.ds(pl.multiple_of(start, size), size)

    local = [
        pltpu.make_async_copy(a, b, lsem.at[i])
        for i, (a, b) in enumerate(
            (
                (x_hbm, x_ref),
                (cache_ref.at[:, :, lanes(y * 256, 256)], kvb.at[y, 0]),
                (cache_ref.at[:, :, lanes(D + y * 256, 256)], kvb.at[y, 1]),
                (wu_ref, up.at[x, c, z]),
                (wd_ref, down.at[x, c, z]),
                (accept_hbm, accept_ref),
                (ga_hbm, ga_ref),
                (gm_hbm, gm_ref),
            )
        )
    ]
    for copy in local:
        copy.start()

    barrier = pltpu.get_barrier_semaphore()
    for k in range(8):
        @pl.when((k > 0) | (from_t != t))
        def _():
            tell(dev_s(k, from_t))

        @pl.when((k > 0) | (from_p != t))
        def _():
            tell(dev_s(k, from_p))
    for k in range(1, NX):
        tell(dev_x(k))
    tell(partner)
    for k in range(1, NY):
        tell(dev_y(k)[1])

    @pl.loop(1, NZ)
    def _(k):
        tell(dev_z(k)[1])

    @pl.loop(0, NZ)
    def _(i):
        zs, ys = 8 * lax.div(i, 8) + 2 * y + lax.rem(lax.div(i, 4), 2), lax.rem(i, 4)

        @pl.when((zs != z) | (ys != y))
        def _():
            tell({"seq": s, "tok": zs * NY + ys})

    @pl.loop(0, NZ)
    def _(i):
        zs, ys = 4 * y + lax.div(i, 4), lax.rem(i, 4)

        @pl.when((zs != z) | (ys != y))
        def _():
            tell({"seq": s, "tok": zs * NY + ys})

    others = (to_t != t).astype(jnp.int32) + (to_kv != y).astype(jnp.int32) + (to_q != y).astype(jnp.int32)
    others += (to_p != t).astype(jnp.int32)
    pl.semaphore_wait(barrier, 14 + NX + (NY - 1) + 3 * (NZ - 1) + others)

    for k in range(8):
        @pl.when((k > 0) | (to_t != t))
        def _():
            put(wq_ref, ws.at[s], WS, dev_s(k, to_t)).start()

        @pl.when((k > 0) | (to_p != t))
        def _():
            put(wkv_ref, ws2.at[s], WS2, dev_s(k, to_p)).start()

    @pl.when(to_t == t)
    def _():
        here(wq_ref, ws.at[s], WS)

    @pl.when(to_p == t)
    def _():
        here(wkv_ref, ws2.at[s], WS2)

    for k in (1, 3, 2):
        yp, dev = dev_y(k)
        put(cache_ref.at[:, :, lanes(yp * 256, 256)], kvb.at[y, 0], CY + k, dev).start()
        put(cache_ref.at[:, :, lanes(D + yp * 256, 256)], kvb.at[y, 1], CY + k, dev).start()
    length = len_ref[0].astype(F32)
    slot_row = lax.broadcasted_iota(jnp.int32, (8, 128), 0)
    limits = jnp.zeros((8, 128), F32)
    for j in range(3):
        page = page_ref[0, j].astype(F32)
        limits = jnp.where(slot_row == j, jnp.where(page >= 0, length - page * 128, 0.0), limits)
    lim[y] = limits
    for k in range(1, NY):
        put(lim.at[y], lim.at[y], LIM, dev_y(k)[1]).start()

    def spread(src, dst, ph, row):
        @pl.loop(1, NZ)
        def _(k):
            put(src, dst, ph, dev_z(k, row)[1]).start()

        @pl.when(row != y)
        def _():
            put(src, dst, ph, dev_z(0, row)[1]).start()

        @pl.when(row == y)
        def _():
            here(src, dst, ph)

    def direct(src, ref, ph):
        for k in (4, 12, 3, 13, 2, 14, 1, 15):
            landed = ph + {4: 1, 12: 2}.get(k, 0)
            put(src, ref.at[x, c, z], ph, dev_z(k)[1], landed).start()

    def relay(ref, ph):
        left, right = lax.rem(z + 12, NZ), lax.rem(z + 4, NZ)
        arrived(ref.at[x, c, left], ph + 1)
        for k in (4, 3, 2, 1):
            put(ref.at[x, c, left], ref.at[x, c, left], ph + 3, dev_z(k)[1]).start()
        arrived(ref.at[x, c, right], ph + 2)
        for k in (13, 14, 15):
            put(ref.at[x, c, right], ref.at[x, c, right], ph + 3, dev_z(k)[1]).start()

    def part(n):
        return (0, 9) if n == 0 else (9, 16)

    def to_x(ref, ph):
        for k in (2, 1, 3):
            put(ref.at[x, c], ref.at[x, c], ph, dev_x(k)).start()

    def ff_to_x(ref, ph, n):
        if n == 0:
            arrived(ref.at[0, 0, pl.ds(0, 6)], ph)
        else:
            arrived(ref.at[0, 0, pl.ds(0, 7)], ph + 3)

        @pl.loop(*part(n))
        def _(i):
            slot = lax.rem(z + 12 + i, NZ)
            for k in (2, 1, 3):
                put(ref.at[x, c, slot], ref.at[x, c, slot], ph + 4 + n, dev_x(k)).start()

    def ff_to_core(ref, ph, n):
        low, high = part(n)
        arrived(ref.at[pl.ds(0, 3), 0, pl.ds(0, high - low)], ph + 4 + n)

        @pl.loop(low, high)
        def _(i):
            slot = lax.rem(z + 12 + i, NZ)
            put(ref.at[:, c, slot], ref.at[:, c, slot], ph + 6 + n, partner).start()

    def ff_ready(ref, ph):
        for n in range(2):
            low, high = part(n)
            arrived(ref.at[:, 0, pl.ds(0, high - low)], ph + 6 + n)

    def to_core(ref, xs, cs):
        arrived(ref.at[pl.ds(0, 3), 0], xs)
        put(ref.at[:, c], ref.at[:, c], cs, partner).start()

    direct(wu_ref, up, UP)
    direct(wd_ref, down, DOWN)
    arrived(ws, WS)
    local[0].wait()
    wq_cols = jnp.concatenate([ws[i] for i in range(8)], axis=1)
    qt[0, z] = dot_nt(wq_cols, x_ref[...]).astype(BF) * jnp.asarray(0.125, BF)

    for k in FAR_FIRST:
        put(qt.at[0, z], qt.at[0, z], PASS + GQZ, dev_z(k)[1]).start()
    arrived(ws2, WS2)
    kv_cols = jnp.concatenate([ws2[i] for i in range(8)], axis=1)
    kv_cols = jnp.concatenate([kv_cols, jnp.zeros((96, D), BF)], axis=0)
    kp[...] = dot_nt(x_ref[...], kv_cols).astype(BF).reshape(NZ, ROWS, 128)
    for k in FAR_FIRST:
        zp, dev = dev_z(k)
        put(kp.at[zp], rkp.at[z], KPZ, dev).start()
    rkp[z] = kp[z]
    spread(wo_ref, ow.at[x, c, lax.rem(z, 4), y], OZ, to_q)

    vt[:, :, 128:144, :] = jnp.ones((NY, 2, 16, KEYS), BF)

    def turn(j):
        for i in range(2):
            for n in range(3):
                vt[j, i, 0:128, 128 * n : 128 * (n + 1)] = jnp.transpose(kvb[j, 1, n, :, 128 * i : 128 * i + 128])

    local[1].wait()
    local[2].wait()
    turn(y)
    local[3].wait()
    local[4].wait()
    relay(up, UP)
    ff_to_x(up, UP, 0)
    relay(down, DOWN)
    ff_to_x(down, DOWN, 0)
    for k in (1, 3, 2):
        src = lax.rem(y + NY - k, NY)
        arrived(kvb.at[src], CY + k)
        turn(src)
    arrived(lim.at[pl.ds(0, 3)], LIM)
    for i in range(5, 8):
        local[i].wait()

    own_rows = pl.ds(pl.multiple_of(z * ROWS, ROWS), ROWS)
    current = x_ref[own_rows, :]

    for p in range(2):
        base = PASS + 6 * p
        if p == 1:
            w_q = jnp.concatenate([qw[i, j].reshape(256, 128) for i in range(4) for j in range(2)], axis=1)
            qz[z] = dot_nt(current, w_q).astype(BF) * jnp.asarray(0.125, BF)

            for k in FAR_FIRST:
                put(qz.at[z], qz.at[z], base + GQZ, dev_z(k)[1]).start()
            arrived(kvw.at[:, 0], KVC)
            arrived(qz.at[pl.ds(0, NZ - 1)], base + GQZ)
            qt[1] = jnp.transpose(qz[...].reshape(TOK, 256)).reshape(NZ, 16, TOK)
        else:
            arrived(qt.at[p, pl.ds(0, NZ - 1)], base + GQZ)

        @pl.loop(0, NY)
        def _(j):
            if p == 0:
                @pl.when(j == 1)
                def _():
                    arrived(ow.at[0, 0], OZ)
                    to_x(ow, OX)

                @pl.when(j == 3)
                def _():
                    ff_to_x(up, UP, 1)

            for i in range(2):
                keys = kvb[j, 0, :, :, 128 * i : 128 * i + 128].reshape(KEYS, 128)
                q_pair = qt[p, 8 * i : 8 * i + 8].reshape(2, 64, TOK)
                none = jnp.zeros((64, TOK), BF)
                both = jnp.concatenate(
                    [
                        jnp.concatenate([q_pair[0], none], axis=1),
                        jnp.concatenate([none, q_pair[1]], axis=1),
                    ],
                    axis=0,
                )
                scores = dot_nn(keys, both)
                offsets = lax.broadcasted_iota(jnp.int32, (128, 2 * TOK), 0).astype(F32)
                masked = jnp.concatenate(
                    [
                        jnp.where(
                            offsets < jnp.concatenate([lim[j, n : n + 1, :]] * 4, axis=1),
                            scores[128 * n : 128 * (n + 1)],
                            MASKED,
                        )
                        for n in range(3)
                    ],
                    axis=0,
                )
                peaks = jnp.maximum(jnp.max(masked, axis=0, keepdims=True), FLOOR_SCORE)
                weights = jnp.exp(masked - peaks).astype(BF)
                summed = dot_nn(vt[j, i], weights)
                po[j, 128 * i : 128 * i + 64, :] = summed[0:64, 0:TOK]
                po[j, 128 * i + 64 : 128 * i + 128, :] = summed[64:128, TOK : 2 * TOK]
                pm[j, 2 * i : 2 * i + 1, :] = peaks[:, 0:TOK]
                pm[j, 2 * i + 1 : 2 * i + 2, :] = peaks[:, TOK : 2 * TOK]
                pm[j, 4 + 2 * i : 5 + 2 * i, :] = summed[128:129, 0:TOK]
                pm[j, 5 + 2 * i : 6 + 2 * i, :] = summed[128:129, TOK : 2 * TOK]

        if p == 0:
            ff_to_x(down, DOWN, 1)
            arrived(rkp.at[pl.ds(0, NZ - 1)], KPZ)
            pieces = [
                sum(pltpu.roll(rkp[4 * i + n].astype(F32), 32 * n, 1) for n in range(1, 4)) + rkp[4 * i].astype(F32)
                for i in range(4)
            ]
            pair = jnp.concatenate(pieces, axis=1)
        else:
            w_pair = jnp.concatenate([kvw[i, j].reshape(512, 128) for i in range(4) for j in range(2)], axis=1)
            pair = dot_nt(current, w_pair)
        row_head = lax.div(lax.broadcasted_iota(jnp.int32, (64, 256), 0), 16)
        lane_head = lax.div(lax.broadcasted_iota(jnp.int32, (64, 256), 1), 64)
        own_head = row_head == lane_head
        k_block = jnp.where(own_head, jnp.concatenate([pair[:, 0:256]] * 4, axis=0), 0.0).astype(BF)
        v_block = jnp.where(own_head, jnp.concatenate([pair[:, 256:512]] * 4, axis=0), 0.0)
        b_scores = dot_nn(k_block, qt[p].reshape(256, TOK)).reshape(4, 16, TOK)
        b_peak = jnp.max(b_scores, axis=1)
        b_weights = jnp.exp(b_scores - b_peak[:, None, :]).astype(BF)
        b_total = jnp.sum(b_weights.astype(F32), axis=1)
        b_sum = dot_nn(jnp.transpose(v_block).astype(BF), b_weights.reshape(64, TOK))

        peaks_y = pm[:, 0:4, :]
        peak = jnp.maximum(jnp.max(peaks_y, axis=0), b_peak)
        scale = jnp.exp(peaks_y - peak[None])
        b_scale = jnp.exp(b_peak - peak)
        total = jnp.sum(scale * pm[:, 4:8, :], axis=0) + b_scale * b_total
        parts = []
        for h in range(4):
            rows = slice(64 * h, 64 * h + 64)
            value = b_sum[rows] * b_scale[h : h + 1]
            for i in range(NY):
                value += po[i, rows, :] * scale[i, h : h + 1]
            parts.append(value)
        tz[p] = jnp.transpose(jnp.concatenate(parts, axis=0)).astype(BF).reshape(NZ, ROWS, 256)
        both = jnp.concatenate([peak, total], axis=0)
        belongs = lax.broadcasted_iota(jnp.int32, (8, 128), 0) == lax.div(
            lax.broadcasted_iota(jnp.int32, (8, 128), 1), ROWS
        )
        steps = [pltpu.roll(both[:, 128 * i : 128 * i + 128], 0, 1, stride=ROWS, stride_axis=0) for i in range(2)]
        for i in range(NZ):
            moved = pltpu.roll(steps[i // 8], (128 - ROWS * (i % 8)) % 128, 1)
            tzm[p, i] = jnp.sum(jnp.where(belongs, moved, 0.0), axis=0, keepdims=True)

        for k in FAR_FIRST:
            zp, dev = dev_z(k)
            put(tzm.at[p, zp], rzm.at[p, z], base + RSZM, dev).start()
            put(tz.at[p, zp], rz.at[p, z], base + RSZ, dev).start()

        rz[p, z] = tz[p, z]
        rzm[p, z] = tzm[p, z]
        if p == 0:
            spread(wkv_ref, kvw.at[x, c, za, zc, y], KVZ, to_kv)
            spread(wq_ref, qw.at[x, c, lax.rem(z, 4), y], QZ, to_q)
            to_core(ow, OX, OC)
            ff_to_core(up, UP, 0)
            ff_to_core(down, DOWN, 0)

        arrived(rzm.at[p, pl.ds(0, NZ - 1)], base + RSZM)
        stats = rzm[p].reshape(NZ, 128)
        scale_z = jnp.exp(stats - jnp.max(stats, axis=0, keepdims=True))
        share = scale_z / jnp.sum(scale_z * pltpu.roll(stats, 64, 1), axis=0, keepdims=True)
        share = jnp.transpose(jnp.concatenate([share, jnp.zeros((128 - NZ, 128), F32)], axis=0))
        arrived(rz.at[p, pl.ds(0, NZ - 1)], base + RSZ)
        lower = lax.broadcasted_iota(jnp.int32, (ROWS, 128), 1) < 64
        halves = [jnp.zeros((ROWS, 128), F32), jnp.zeros((ROWS, 128), F32)]
        for i in range(NZ):
            for n in range(2):
                low = jnp.broadcast_to(share[32 * n : 32 * n + 16, i : i + 1], (ROWS, 128))
                high = jnp.broadcast_to(share[32 * n + 16 : 32 * n + 32, i : i + 1], (ROWS, 128))
                halves[n] += jnp.where(lower, low, high) * rz[p, i, :, 128 * n : 128 * n + 128].astype(F32)
        att[p, y] = jnp.concatenate(halves, axis=1).astype(BF)
        for k in range(1, NY):
            put(att.at[p, y], att.at[p, y], base + GAY, dev_y(k)[1]).start()
        if p == 0:
            ff_to_core(up, UP, 1)
            arrived(ow.at[:, 0], OC)
        arrived(att.at[p, pl.ds(0, 3)], base + GAY)

        w_o = jnp.concatenate([ow[i, j].reshape(256, 128) for i in range(4) for j in range(2)], axis=1)
        ob[p, y] = dot_nt(jnp.concatenate([att[p, i] for i in range(NY)], axis=1), w_o)
        for k in range(1, NY):
            put(ob.at[p, y], ob.at[p, y], base + GOY, dev_y(k)[1]).start()
        if p == 0:
            ff_to_core(down, DOWN, 1)
            arrived(kvw.at[0, 0], KVZ)
            to_x(kvw, KVX)
            arrived(qw.at[0, 0], QZ)
            to_x(qw, QX)
        arrived(ob.at[p, pl.ds(0, 3)], base + GOY)
        residual = current.astype(F32) + jnp.concatenate([ob[p, i] for i in range(NY)], axis=1)
        settled = layer_norm(residual, ga_ref[...]).astype(BF)

        if p == 0:
            ff_ready(up, UP)
        w_u = jnp.concatenate([up[i, j].reshape(D, 128) for i in range(4) for j in range(2)], axis=1)
        product = dot_nt(settled, w_u)
        hidden = (0.5 * product * (1.0 + lax.erf(product * (0.5**0.5)))).astype(BF)
        if p == 0:
            ff_ready(down, DOWN)
        w_d = jnp.concatenate([down[i, j].reshape(D, 128) for i in range(4) for j in range(2)], axis=1)
        fp[p, y] = dot_nn(hidden, w_d).astype(BF)
        for k in range(1, NY):
            put(fp.at[p, y], fp.at[p, y], base + RFY, dev_y(k)[1]).start()
        if p == 0:
            to_core(qw, QX, QC)
            to_core(kvw, KVX, KVC)
            arrived(qw.at[:, 0], QC)
        arrived(fp.at[p, pl.ds(0, 3)], base + RFY)
        projected = fp[p, 0].astype(F32) + fp[p, 1].astype(F32) + fp[p, 2].astype(F32) + fp[p, 3].astype(F32)
        finished = layer_norm(settled.astype(F32) + projected, gm_ref[...])
        own_token = lax.broadcasted_iota(jnp.int32, (ROWS, TOK), 1) == z * ROWS + lax.broadcasted_iota(
            jnp.int32, (ROWS, TOK), 0
        )
        taken = jnp.sum(jnp.where(own_token, accept_ref[p].astype(F32), 0.0), axis=1, keepdims=True) > 0.5
        current = jnp.where(taken, finished, current.astype(F32)).astype(BF)

    fin[...] = current
    quarter = lanes(y * 256, 256)
    fz[z] = fin[:, quarter]

    def hand_on(zp):
        for k in range(1, NY):
            put(fz.at[zp], out_ref.at[zp, :, quarter], FIN_Y, dev_y(k)[1]).start()

    def in_turn(i):
        near = lax.div(i, 2) + 1
        return jnp.where(lax.rem(i, 2) == 0, near, NZ - near)

    @pl.loop(0, NZ - 1)
    def _(i):
        k = in_turn(i)
        put(fz.at[z], fz.at[z], FIN_Z + k, dev_z(k)[1]).start()

    hand_on(z)

    @pl.loop(0, NZ - 1)
    def _(i):
        k = in_turn(i)
        zp = lax.rem(z + NZ - k, NZ)
        arrived(fz.at[zp], FIN_Z + k)
        hand_on(zp)

    out_ref[:, :, quarter] = fz[...]
    arrived(out_ref.at[:, :, pl.ds(0, 768)], FIN_Y)

    def sent_but_own(ref, axis_end, ph, own):
        @pl.when(own)
        def _():
            sent(ref.at[pl.ds(0, axis_end - 1)], ph)

        @pl.when(jnp.logical_not(own))
        def _():
            sent(ref.at[pl.ds(0, axis_end)], ph)

    sent_but_own(ws, 8, WS, to_t == t)
    sent_but_own(qz, NZ, KVZ, to_kv == y)
    sent_but_own(hold, NZ, OZ, to_q == y)
    sent_but_own(hold, NZ, QZ, to_q == y)
    sent_but_own(ws2, 8, WS2, to_p == t)
    sent(rkp.at[pl.ds(0, NZ - 1)], KPZ)
    for ref, xs, cs in ((qw, QX, QC), (kvw, KVX, KVC), (ow, OX, OC)):
        sent(ref.at[pl.ds(0, 3), 0], xs)
        sent(ref.at[:, 0], cs)
    for ph in (UP, DOWN):
        sent(up.at[0, 0, pl.ds(0, 8)], ph)
        sent(up.at[0, 0, pl.ds(0, 7)], ph + 3)
        for n in range(2):
            low, high = part(n)
            sent(up.at[pl.ds(0, 3), 0, pl.ds(0, high - low)], ph + 4 + n)
            sent(up.at[:, 0, pl.ds(0, high - low)], ph + 6 + n)
    for k in range(1, NY):
        sent(kvb.at[0], CY + k)
    sent(lim.at[pl.ds(0, 3)], LIM)
    for p in range(2):
        base = PASS + 6 * p
        sent(qz.at[pl.ds(0, NZ - 1)], base + GQZ)
        sent(rz.at[p, pl.ds(0, NZ - 1)], base + RSZ)
        sent(rzm.at[p, pl.ds(0, NZ - 1)], base + RSZM)
        sent(att.at[p, pl.ds(0, 3)], base + GAY)
        sent(ob.at[p, pl.ds(0, 3)], base + GOY)
        sent(fp.at[p, pl.ds(0, 3)], base + RFY)

    @pl.loop(1, NZ)
    def _(k):
        sent(fz.at[0], FIN_Z + k)

    sent(out_ref.at[:, :, pl.ds(0, 768)], FIN_Y)


def shards(
    block_in, accept, cache_len, slot_page, cache_kv, w_query, w_key_value, w_out, gain_attn, w_up, w_down, gain_mlp
):
    smem = pl.BlockSpec(memory_space=pltpu.SMEM)
    result = pl.pallas_call(
        kernel,
        out_shape=jax.ShapeDtypeStruct((NZ, ROWS, D), BF),
        in_specs=[smem, smem] + [pl.BlockSpec(memory_space=pltpu.HBM)] * 10,
        out_specs=pl.BlockSpec(memory_space=pltpu.VMEM),
        scratch_shapes=[
            pltpu.VMEM((TOK, D), BF),
            pltpu.VMEM((2, 1, TOK), jnp.int32),
            pltpu.VMEM((1, D), F32),
            pltpu.VMEM((1, D), F32),
            pltpu.VMEM((NY, 2, 3, 128, 256), BF),
            pltpu.VMEM((NY, 2, 144, KEYS), BF),
            pltpu.VMEM((NY, 8, 128), F32),
            pltpu.VMEM((8, 16, 128), BF),
            pltpu.VMEM((8, 32, 128), BF),
            pltpu.VMEM((NZ, ROWS, 128), BF),
            pltpu.VMEM((NZ, ROWS, 128), BF),
            pltpu.VMEM((4, 2, 4, 4, 16, 128), BF),
            pltpu.VMEM((4, 2, 2, 2, 4, 32, 128), BF),
            pltpu.VMEM((4, 2, 4, 4, 16, 128), BF),
            pltpu.VMEM((4, 2, NZ, 64, 128), BF),
            pltpu.VMEM((4, 2, NZ, 64, 128), BF),
            pltpu.VMEM((NZ, 16, 128), BF),
            pltpu.VMEM((NZ, ROWS, 256), BF),
            pltpu.VMEM((2, NZ, 16, TOK), BF),
            pltpu.VMEM((NY, 256, TOK), F32),
            pltpu.VMEM((NY, 8, TOK), F32),
            pltpu.VMEM((2, NZ, ROWS, 256), BF),
            pltpu.VMEM((2, NZ, 1, 128), F32),
            pltpu.VMEM((2, NZ, ROWS, 256), BF),
            pltpu.VMEM((2, NZ, 1, 128), F32),
            pltpu.VMEM((2, NY, ROWS, 256), BF),
            pltpu.VMEM((2, NY, ROWS, 256), F32),
            pltpu.VMEM((2, NY, ROWS, D), BF),
            pltpu.VMEM((ROWS, D), BF),
            pltpu.VMEM((NZ, ROWS, 256), BF),
            pltpu.SemaphoreType.DMA((N_SEM,)),
            pltpu.SemaphoreType.DMA((N_SEM,)),
            pltpu.SemaphoreType.DMA((8,)),
        ],
        compiler_params=pltpu.CompilerParams(
            collective_id=0, has_side_effects=True, vmem_limit_bytes=63 * 1024 * 1024
        ),
    )(
        cache_len,
        slot_page,
        block_in[0],
        accept,
        cache_kv[0],
        w_query.T,
        w_key_value.T,
        w_out.T,
        w_up.T,
        w_down,
        gain_attn[None],
        gain_mlp[None],
    )
    return result.reshape(1, TOK, D)


def solution(mesh):
    in_specs = (
        P("seq", None, None),
        P(None, "seq", None),
        P("seq"),
        P("seq", "tok"),
        P("seq", "tok", None, None),
        P("seq", "tok"),
        P("seq", "tok"),
        P("seq", "tok"),
        P(),
        P("seq", "tok"),
        P("tok", "seq"),
        P(),
    )
    out_specs = P("seq", None, None)
    return jax.shard_map(shards, mesh=mesh, in_specs=in_specs, out_specs=out_specs, check_vma=False)
```

```python
import jax
import jax.numpy as jnp
from jax import lax
from jax.experimental import pallas as pl
from jax.experimental.pallas import tpu as pltpu
from jax.sharding import PartitionSpec as P

MESH = pl.DeviceIdType.MESH
BF = jnp.bfloat16
F32 = jnp.float32

D = 1024
TOK = 256
NZ, NY, NX = 16, 4, 4
ROWS = TOK // NZ
KEYS = 384
EPSILON = 1e-05
FLOOR_SCORE = -1e30
MASKED = -3e38

(WS, KVZ, OZ, QZ, KVX, OX, QX, KVC, OC, QC, WS2, KPZ, LIM) = range(13)
CY = 13
UP, DOWN = 17, 25
PASS = 33
FAR_FIRST = (8, 7, 9, 6, 10, 5, 11, 4, 12, 3, 13, 2, 14, 1, 15)
(GQZ, RSZ, RSZM, GAY, GOY, RFY) = range(6)
FIN_Y, FIN_Z = PASS + 12, PASS + 12
N_SEM = PASS + 28


def dot_nn(a, b):
    return lax.dot_general(a, b, (((1,), (0,)), ((), ())), preferred_element_type=F32)


def dot_nt(a, b):
    return lax.dot_general(a, b, (((1,), (1,)), ((), ())), preferred_element_type=F32)


def layer_norm(values, gain):
    average = jnp.mean(values, axis=-1, keepdims=True)
    centered = values - average
    variance = jnp.mean(centered * centered, axis=-1, keepdims=True)
    return centered * lax.rsqrt(variance + EPSILON) * gain


def kernel(
    len_ref, page_ref, x_hbm, accept_hbm, cache_ref, wq_ref, wkv_ref, wo_ref, wu_ref, wd_ref, ga_hbm, gm_hbm,
    out_ref,
    x_ref, accept_ref, ga_ref, gm_ref, kvb, vt, lim, ws, ws2, kp, rkp, qw, kvw, ow, up, down,
    hold, qz, qt, po, pm, tz, tzm, rz, rzm, att, ob, fp, fin, fz,
    ssem, rsem, lsem,
):
    s, t = lax.axis_index("seq"), lax.axis_index("tok")
    x, c = lax.div(s, 2), lax.rem(s, 2)
    z, y = lax.div(t, NY), lax.rem(t, NY)
    za, zc = lax.div(z, 8), lax.rem(z, 2)
    to_kv = lax.div(lax.rem(z, 8), 2)
    to_q = lax.div(z, 4)
    to_t = lax.rem(t, NZ) * NY + lax.div(t, NZ)
    from_t = (NY * y + lax.div(z, NY)) * NY + lax.rem(z, NY)
    to_p = (lax.rem(t, 8) + 8 * lax.div(t, 32)) * NY + lax.rem(lax.div(t, 8), 4)
    from_p = 8 * y + z + 24 * za

    def dev_z(k, row=None):
        zp = lax.rem(z + k, NZ)
        return zp, {"seq": s, "tok": zp * NY + (y if row is None else row)}

    def dev_y(k):
        yp = lax.rem(y + k, NY)
        return yp, {"seq": s, "tok": z * NY + yp}

    def dev_s(k, tok):
        return {"seq": lax.rem(s + k, 2 * NX), "tok": tok}

    def dev_x(k):
        return {"seq": lax.rem(x + k, NX) * 2 + c, "tok": t}

    partner = {"seq": x * 2 + 1 - c, "tok": t}

    def put(src, dst, ph, dev, rph=None):
        return pltpu.make_async_remote_copy(
            src_ref=src,
            dst_ref=dst,
            send_sem=ssem.at[ph],
            recv_sem=rsem.at[ph if rph is None else rph],
            device_id=dev,
            device_id_type=MESH,
        )

    def arrived(view, ph):
        put(view, view, ph, partner).wait_recv()

    def sent(view, ph):
        put(view, view, ph, partner).wait_send()

    def here(src, dst, ph):
        pltpu.make_async_copy(src, dst, rsem.at[ph]).start()

    def tell(dev):
        pl.semaphore_signal(barrier, inc=1, device_id=dev, device_id_type=MESH)

    def lanes(start, size):
        return pl.ds(pl.multiple_of(start, size), size)

    barrier = pltpu.get_barrier_semaphore()
    for k in range(8):
        @pl.when((k > 0) | (from_t != t))
        def _():
            tell(dev_s(k, from_t))

        @pl.when((k > 0) | (from_p != t))
        def _():
            tell(dev_s(k, from_p))
    for k in range(1, NX):
        tell(dev_x(k))
    tell(partner)
    for k in range(1, NY):
        tell(dev_y(k)[1])

    @pl.loop(1, NZ)
    def _(k):
        tell(dev_z(k)[1])

    @pl.loop(0, NZ)
    def _(i):
        zs, ys = 8 * lax.div(i, 8) + 2 * y + lax.rem(lax.div(i, 4), 2), lax.rem(i, 4)

        @pl.when((zs != z) | (ys != y))
        def _():
            tell({"seq": s, "tok": zs * NY + ys})

    @pl.loop(0, NZ)
    def _(i):
        zs, ys = 4 * y + lax.div(i, 4), lax.rem(i, 4)

        @pl.when((zs != z) | (ys != y))
        def _():
            tell({"seq": s, "tok": zs * NY + ys})

    local = [
        pltpu.make_async_copy(a, b, lsem.at[i])
        for i, (a, b) in enumerate(
            (
                (x_hbm, x_ref),
                (cache_ref.at[:, :, lanes(y * 256, 256)], kvb.at[y, 0]),
                (cache_ref.at[:, :, lanes(D + y * 256, 256)], kvb.at[y, 1]),
                (wu_ref, up.at[x, c, z]),
                (wd_ref, down.at[x, c, z]),
                (accept_hbm, accept_ref),
                (ga_hbm, ga_ref),
                (gm_hbm, gm_ref),
            )
        )
    ]
    for copy in local:
        copy.start()

    others = (to_t != t).astype(jnp.int32) + (to_kv != y).astype(jnp.int32) + (to_q != y).astype(jnp.int32)
    others += (to_p != t).astype(jnp.int32)
    pl.semaphore_wait(barrier, 14 + NX + (NY - 1) + 3 * (NZ - 1) + others)

    for k in range(8):
        @pl.when((k > 0) | (to_t != t))
        def _():
            put(wq_ref, ws.at[s], WS, dev_s(k, to_t)).start()

        @pl.when((k > 0) | (to_p != t))
        def _():
            put(wkv_ref, ws2.at[s], WS2, dev_s(k, to_p)).start()

    @pl.when(to_t == t)
    def _():
        here(wq_ref, ws.at[s], WS)

    @pl.when(to_p == t)
    def _():
        here(wkv_ref, ws2.at[s], WS2)

    for k in (1, 3, 2):
        yp, dev = dev_y(k)
        put(cache_ref.at[:, :, lanes(yp * 256, 256)], kvb.at[y, 0], CY + k, dev).start()
        put(cache_ref.at[:, :, lanes(D + yp * 256, 256)], kvb.at[y, 1], CY + k, dev).start()
    length = len_ref[0].astype(F32)
    slot_row = lax.broadcasted_iota(jnp.int32, (8, 128), 0)
    limits = jnp.zeros((8, 128), F32)
    for j in range(3):
        page = page_ref[0, j].astype(F32)
        limits = jnp.where(slot_row == j, jnp.where(page >= 0, length - page * 128, 0.0), limits)
    lim[y] = limits
    for k in range(1, NY):
        put(lim.at[y], lim.at[y], LIM, dev_y(k)[1]).start()

    def spread(src, dst, ph, row):
        @pl.loop(1, NZ)
        def _(k):
            put(src, dst, ph, dev_z(k, row)[1]).start()

        @pl.when(row != y)
        def _():
            put(src, dst, ph, dev_z(0, row)[1]).start()

        @pl.when(row == y)
        def _():
            here(src, dst, ph)

    def direct(src, ref, ph):
        for k in (4, 12, 3, 13, 2, 14, 1, 15):
            landed = ph + {4: 1, 12: 2}.get(k, 0)
            put(src, ref.at[x, c, z], ph, dev_z(k)[1], landed).start()

    def relay(ref, ph):
        left, right = lax.rem(z + 12, NZ), lax.rem(z + 4, NZ)
        arrived(ref.at[x, c, left], ph + 1)
        for k in (4, 3, 2, 1):
            put(ref.at[x, c, left], ref.at[x, c, left], ph + 3, dev_z(k)[1]).start()
        arrived(ref.at[x, c, right], ph + 2)
        for k in (13, 14, 15):
            put(ref.at[x, c, right], ref.at[x, c, right], ph + 3, dev_z(k)[1]).start()

    def part(n):
        return (0, 9) if n == 0 else (9, 16)

    def to_x(ref, ph):
        for k in (2, 1, 3):
            put(ref.at[x, c], ref.at[x, c], ph, dev_x(k)).start()

    def ff_to_x(ref, ph, n):
        if n == 0:
            arrived(ref.at[0, 0, pl.ds(0, 6)], ph)
        else:
            arrived(ref.at[0, 0, pl.ds(0, 7)], ph + 3)

        @pl.loop(*part(n))
        def _(i):
            slot = lax.rem(z + 12 + i, NZ)
            for k in (2, 1, 3):
                put(ref.at[x, c, slot], ref.at[x, c, slot], ph + 4 + n, dev_x(k)).start()

    def ff_to_core(ref, ph, n):
        low, high = part(n)
        arrived(ref.at[pl.ds(0, 3), 0, pl.ds(0, high - low)], ph + 4 + n)

        @pl.loop(low, high)
        def _(i):
            slot = lax.rem(z + 12 + i, NZ)
            put(ref.at[:, c, slot], ref.at[:, c, slot], ph + 6 + n, partner).start()

    def ff_ready(ref, ph):
        for n in range(2):
            low, high = part(n)
            arrived(ref.at[:, 0, pl.ds(0, high - low)], ph + 6 + n)

    def to_core(ref, xs, cs):
        arrived(ref.at[pl.ds(0, 3), 0], xs)
        put(ref.at[:, c], ref.at[:, c], cs, partner).start()

    direct(wu_ref, up, UP)
    direct(wd_ref, down, DOWN)
    arrived(ws, WS)
    local[0].wait()
    wq_cols = jnp.concatenate([ws[i] for i in range(8)], axis=1)
    qt[0, z] = dot_nt(wq_cols, x_ref[...]).astype(BF) * jnp.asarray(0.125, BF)

    for k in FAR_FIRST:
        put(qt.at[0, z], qt.at[0, z], PASS + GQZ, dev_z(k)[1]).start()
    arrived(ws2, WS2)
    kv_cols = jnp.concatenate([ws2[i] for i in range(8)], axis=1)
    kv_cols = jnp.concatenate([kv_cols, jnp.zeros((96, D), BF)], axis=0)
    kp[...] = dot_nt(x_ref[...], kv_cols).astype(BF).reshape(NZ, ROWS, 128)
    for k in FAR_FIRST:
        zp, dev = dev_z(k)
        put(kp.at[zp], rkp.at[z], KPZ, dev).start()
    rkp[z] = kp[z]

    vt[:, :, 128:144, :] = jnp.ones((NY, 2, 16, KEYS), BF)

    def turn(j):
        for i in range(2):
            for n in range(3):
                vt[j, i, 0:128, 128 * n : 128 * (n + 1)] = jnp.transpose(kvb[j, 1, n, :, 128 * i : 128 * i + 128])

    local[1].wait()
    local[2].wait()
    turn(y)
    local[3].wait()
    local[4].wait()
    relay(up, UP)
    ff_to_x(up, UP, 0)
    relay(down, DOWN)
    ff_to_x(down, DOWN, 0)
    for k in (1, 3, 2):
        src = lax.rem(y + NY - k, NY)
        arrived(kvb.at[src], CY + k)
        turn(src)
    arrived(lim.at[pl.ds(0, 3)], LIM)
    for i in range(5, 8):
        local[i].wait()

    own_rows = pl.ds(pl.multiple_of(z * ROWS, ROWS), ROWS)
    current = x_ref[own_rows, :]

    for p in range(2):
        base = PASS + 6 * p
        if p == 1:
            w_q = jnp.concatenate([qw[i, j].reshape(256, 128) for i in range(4) for j in range(2)], axis=1)
            qz[z] = dot_nt(current, w_q).astype(BF) * jnp.asarray(0.125, BF)

            for k in FAR_FIRST:
                put(qz.at[z], qz.at[z], base + GQZ, dev_z(k)[1]).start()
            arrived(qz.at[pl.ds(0, NZ - 1)], base + GQZ)
            to_core(kvw, KVX, KVC)
            qt[1] = jnp.transpose(qz[...].reshape(TOK, 256)).reshape(NZ, 16, TOK)
        else:
            arrived(qt.at[p, pl.ds(0, NZ - 1)], base + GQZ)
            spread(wo_ref, ow.at[x, c, lax.rem(z, 4), y], OZ, to_q)

        @pl.loop(0, NY)
        def _(j):
            if p == 0:
                @pl.when(j == 3)
                def _():
                    ff_to_x(up, UP, 1)

            for i in range(2):
                keys = kvb[j, 0, :, :, 128 * i : 128 * i + 128].reshape(KEYS, 128)
                q_pair = qt[p, 8 * i : 8 * i + 8].reshape(2, 64, TOK)
                none = jnp.zeros((64, TOK), BF)
                both = jnp.concatenate(
                    [
                        jnp.concatenate([q_pair[0], none], axis=1),
                        jnp.concatenate([none, q_pair[1]], axis=1),
                    ],
                    axis=0,
                )
                scores = dot_nn(keys, both)
                offsets = lax.broadcasted_iota(jnp.int32, (128, 2 * TOK), 0).astype(F32)
                masked = jnp.concatenate(
                    [
                        jnp.where(
                            offsets < jnp.concatenate([lim[j, n : n + 1, :]] * 4, axis=1),
                            scores[128 * n : 128 * (n + 1)],
                            MASKED,
                        )
                        for n in range(3)
                    ],
                    axis=0,
                )
                peaks = jnp.maximum(jnp.max(masked, axis=0, keepdims=True), FLOOR_SCORE)
                weights = jnp.exp(masked - peaks).astype(BF)
                summed = dot_nn(vt[j, i], weights)
                po[j, 128 * i : 128 * i + 64, :] = summed[0:64, 0:TOK]
                po[j, 128 * i + 64 : 128 * i + 128, :] = summed[64:128, TOK : 2 * TOK]
                pm[j, 2 * i : 2 * i + 1, :] = peaks[:, 0:TOK]
                pm[j, 2 * i + 1 : 2 * i + 2, :] = peaks[:, TOK : 2 * TOK]
                pm[j, 4 + 2 * i : 5 + 2 * i, :] = summed[128:129, 0:TOK]
                pm[j, 5 + 2 * i : 6 + 2 * i, :] = summed[128:129, TOK : 2 * TOK]

        if p == 0:
            ff_to_x(down, DOWN, 1)
            arrived(rkp.at[pl.ds(0, NZ - 1)], KPZ)
            pieces = [
                sum(pltpu.roll(rkp[4 * i + n].astype(F32), 32 * n, 1) for n in range(1, 4)) + rkp[4 * i].astype(F32)
                for i in range(4)
            ]
            pair = jnp.concatenate(pieces, axis=1)
        else:
            arrived(kvw.at[:, 0], KVC)
            w_pair = jnp.concatenate([kvw[i, j].reshape(512, 128) for i in range(4) for j in range(2)], axis=1)
            pair = dot_nt(current, w_pair)
        row_head = lax.div(lax.broadcasted_iota(jnp.int32, (64, 256), 0), 16)
        lane_head = lax.div(lax.broadcasted_iota(jnp.int32, (64, 256), 1), 64)
        own_head = row_head == lane_head
        k_block = jnp.where(own_head, jnp.concatenate([pair[:, 0:256]] * 4, axis=0), 0.0).astype(BF)
        v_block = jnp.where(own_head, jnp.concatenate([pair[:, 256:512]] * 4, axis=0), 0.0)
        b_scores = dot_nn(k_block, qt[p].reshape(256, TOK)).reshape(4, 16, TOK)
        b_peak = jnp.max(b_scores, axis=1)
        b_weights = jnp.exp(b_scores - b_peak[:, None, :]).astype(BF)
        b_total = jnp.sum(b_weights.astype(F32), axis=1)
        b_sum = dot_nn(jnp.transpose(v_block).astype(BF), b_weights.reshape(64, TOK))

        peaks_y = pm[:, 0:4, :]
        peak = jnp.maximum(jnp.max(peaks_y, axis=0), b_peak)
        scale = jnp.exp(peaks_y - peak[None])
        b_scale = jnp.exp(b_peak - peak)
        total = jnp.sum(scale * pm[:, 4:8, :], axis=0) + b_scale * b_total
        parts = []
        for h in range(4):
            rows = slice(64 * h, 64 * h + 64)
            value = b_sum[rows] * b_scale[h : h + 1]
            for i in range(NY):
                value += po[i, rows, :] * scale[i, h : h + 1]
            parts.append(value)
        tz[p] = jnp.transpose(jnp.concatenate(parts, axis=0)).astype(BF).reshape(NZ, ROWS, 256)
        both = jnp.concatenate([peak, total], axis=0)
        belongs = lax.broadcasted_iota(jnp.int32, (8, 128), 0) == lax.div(
            lax.broadcasted_iota(jnp.int32, (8, 128), 1), ROWS
        )
        steps = [pltpu.roll(both[:, 128 * i : 128 * i + 128], 0, 1, stride=ROWS, stride_axis=0) for i in range(2)]
        for i in range(NZ):
            moved = pltpu.roll(steps[i // 8], (128 - ROWS * (i % 8)) % 128, 1)
            tzm[p, i] = jnp.sum(jnp.where(belongs, moved, 0.0), axis=0, keepdims=True)

        for k in FAR_FIRST:
            zp, dev = dev_z(k)
            put(tzm.at[p, zp], rzm.at[p, z], base + RSZM, dev).start()
            put(tz.at[p, zp], rz.at[p, z], base + RSZ, dev).start()

        rz[p, z] = tz[p, z]
        rzm[p, z] = tzm[p, z]
        if p == 0:
            arrived(ow.at[0, 0], OZ)
            to_x(ow, OX)
            ff_to_core(up, UP, 0)
            ff_to_core(down, DOWN, 0)

        arrived(rzm.at[p, pl.ds(0, NZ - 1)], base + RSZM)
        stats = rzm[p].reshape(NZ, 128)
        scale_z = jnp.exp(stats - jnp.max(stats, axis=0, keepdims=True))
        share = scale_z / jnp.sum(scale_z * pltpu.roll(stats, 64, 1), axis=0, keepdims=True)
        share = jnp.transpose(jnp.concatenate([share, jnp.zeros((128 - NZ, 128), F32)], axis=0))
        arrived(rz.at[p, pl.ds(0, NZ - 1)], base + RSZ)
        if p == 0:
            spread(wq_ref, qw.at[x, c, lax.rem(z, 4), y], QZ, to_q)
            spread(wkv_ref, kvw.at[x, c, za, zc, y], KVZ, to_kv)
            to_core(ow, OX, OC)
        lower = lax.broadcasted_iota(jnp.int32, (ROWS, 128), 1) < 64
        halves = [jnp.zeros((ROWS, 128), F32), jnp.zeros((ROWS, 128), F32)]
        for i in range(NZ):
            for n in range(2):
                low = jnp.broadcast_to(share[32 * n : 32 * n + 16, i : i + 1], (ROWS, 128))
                high = jnp.broadcast_to(share[32 * n + 16 : 32 * n + 32, i : i + 1], (ROWS, 128))
                halves[n] += jnp.where(lower, low, high) * rz[p, i, :, 128 * n : 128 * n + 128].astype(F32)
        att[p, y] = jnp.concatenate(halves, axis=1).astype(BF)
        for k in range(1, NY):
            put(att.at[p, y], att.at[p, y], base + GAY, dev_y(k)[1]).start()
        if p == 0:
            ff_to_core(up, UP, 1)
            arrived(ow.at[:, 0], OC)
        arrived(att.at[p, pl.ds(0, 3)], base + GAY)

        w_o = jnp.concatenate([ow[i, j].reshape(256, 128) for i in range(4) for j in range(2)], axis=1)
        ob[p, y] = dot_nt(jnp.concatenate([att[p, i] for i in range(NY)], axis=1), w_o)
        for k in range(1, NY):
            put(ob.at[p, y], ob.at[p, y], base + GOY, dev_y(k)[1]).start()
        if p == 0:
            ff_to_core(down, DOWN, 1)
            arrived(qw.at[0, 0], QZ)
            to_x(qw, QX)
        arrived(ob.at[p, pl.ds(0, 3)], base + GOY)
        residual = current.astype(F32) + jnp.concatenate([ob[p, i] for i in range(NY)], axis=1)
        settled = layer_norm(residual, ga_ref[...]).astype(BF)

        if p == 0:
            ff_ready(up, UP)
        w_u = jnp.concatenate([up[i, j].reshape(D, 128) for i in range(4) for j in range(2)], axis=1)
        product = dot_nt(settled, w_u)
        hidden = (0.5 * product * (1.0 + lax.erf(product * (0.5**0.5)))).astype(BF)
        if p == 0:
            ff_ready(down, DOWN)
        w_d = jnp.concatenate([down[i, j].reshape(D, 128) for i in range(4) for j in range(2)], axis=1)
        fp[p, y] = dot_nn(hidden, w_d).astype(BF)
        for k in range(1, NY):
            put(fp.at[p, y], fp.at[p, y], base + RFY, dev_y(k)[1]).start()
        if p == 0:
            to_core(qw, QX, QC)
            arrived(kvw.at[0, 0], KVZ)
            to_x(kvw, KVX)
            arrived(qw.at[:, 0], QC)
        arrived(fp.at[p, pl.ds(0, 3)], base + RFY)
        projected = fp[p, 0].astype(F32) + fp[p, 1].astype(F32) + fp[p, 2].astype(F32) + fp[p, 3].astype(F32)
        finished = layer_norm(settled.astype(F32) + projected, gm_ref[...])
        own_token = lax.broadcasted_iota(jnp.int32, (ROWS, TOK), 1) == z * ROWS + lax.broadcasted_iota(
            jnp.int32, (ROWS, TOK), 0
        )
        taken = jnp.sum(jnp.where(own_token, accept_ref[p].astype(F32), 0.0), axis=1, keepdims=True) > 0.5
        current = jnp.where(taken, finished, current.astype(F32)).astype(BF)

    fin[...] = current
    quarter = lanes(y * 256, 256)
    fz[z] = fin[:, quarter]

    def hand_on(zp):
        for k in range(1, NY):
            put(fz.at[zp], out_ref.at[zp, :, quarter], FIN_Y, dev_y(k)[1]).start()

    def in_turn(i):
        near = lax.div(i, 2) + 1
        return jnp.where(lax.rem(i, 2) == 0, near, NZ - near)

    @pl.loop(0, NZ - 1)
    def _(i):
        k = in_turn(i)
        put(fz.at[z], fz.at[z], FIN_Z + k, dev_z(k)[1]).start()

    hand_on(z)

    @pl.loop(0, NZ - 1)
    def _(i):
        k = in_turn(i)
        zp = lax.rem(z + NZ - k, NZ)
        arrived(fz.at[zp], FIN_Z + k)
        hand_on(zp)

    out_ref[:, :, quarter] = fz[...]
    arrived(out_ref.at[:, :, pl.ds(0, 768)], FIN_Y)

    def sent_but_own(ref, axis_end, ph, own):
        @pl.when(own)
        def _():
            sent(ref.at[pl.ds(0, axis_end - 1)], ph)

        @pl.when(jnp.logical_not(own))
        def _():
            sent(ref.at[pl.ds(0, axis_end)], ph)

    sent_but_own(ws, 8, WS, to_t == t)
    sent_but_own(qz, NZ, KVZ, to_kv == y)
    sent_but_own(hold, NZ, OZ, to_q == y)
    sent_but_own(hold, NZ, QZ, to_q == y)
    sent_but_own(ws2, 8, WS2, to_p == t)
    sent(rkp.at[pl.ds(0, NZ - 1)], KPZ)
    for ref, xs, cs in ((qw, QX, QC), (kvw, KVX, KVC), (ow, OX, OC)):
        sent(ref.at[pl.ds(0, 3), 0], xs)
        sent(ref.at[:, 0], cs)
    for ph in (UP, DOWN):
        sent(up.at[0, 0, pl.ds(0, 8)], ph)
        sent(up.at[0, 0, pl.ds(0, 7)], ph + 3)
        for n in range(2):
            low, high = part(n)
            sent(up.at[pl.ds(0, 3), 0, pl.ds(0, high - low)], ph + 4 + n)
            sent(up.at[:, 0, pl.ds(0, high - low)], ph + 6 + n)
    for k in range(1, NY):
        sent(kvb.at[0], CY + k)
    sent(lim.at[pl.ds(0, 3)], LIM)
    for p in range(2):
        base = PASS + 6 * p
        sent(qz.at[pl.ds(0, NZ - 1)], base + GQZ)
        sent(rz.at[p, pl.ds(0, NZ - 1)], base + RSZ)
        sent(rzm.at[p, pl.ds(0, NZ - 1)], base + RSZM)
        sent(att.at[p, pl.ds(0, 3)], base + GAY)
        sent(ob.at[p, pl.ds(0, 3)], base + GOY)
        sent(fp.at[p, pl.ds(0, 3)], base + RFY)

    @pl.loop(1, NZ)
    def _(k):
        sent(fz.at[0], FIN_Z + k)

    sent(out_ref.at[:, :, pl.ds(0, 768)], FIN_Y)


def shards(
    block_in, accept, cache_len, slot_page, cache_kv, w_query, w_key_value, w_out, gain_attn, w_up, w_down, gain_mlp
):
    smem = pl.BlockSpec(memory_space=pltpu.SMEM)
    result = pl.pallas_call(
        kernel,
        out_shape=jax.ShapeDtypeStruct((NZ, ROWS, D), BF),
        in_specs=[smem, smem] + [pl.BlockSpec(memory_space=pltpu.HBM)] * 10,
        out_specs=pl.BlockSpec(memory_space=pltpu.VMEM),
        scratch_shapes=[
            pltpu.VMEM((TOK, D), BF),
            pltpu.VMEM((2, 1, TOK), jnp.int32),
            pltpu.VMEM((1, D), F32),
            pltpu.VMEM((1, D), F32),
            pltpu.VMEM((NY, 2, 3, 128, 256), BF),
            pltpu.VMEM((NY, 2, 144, KEYS), BF),
            pltpu.VMEM((NY, 8, 128), F32),
            pltpu.VMEM((8, 16, 128), BF),
            pltpu.VMEM((8, 32, 128), BF),
            pltpu.VMEM((NZ, ROWS, 128), BF),
            pltpu.VMEM((NZ, ROWS, 128), BF),
            pltpu.VMEM((4, 2, 4, 4, 16, 128), BF),
            pltpu.VMEM((4, 2, 2, 2, 4, 32, 128), BF),
            pltpu.VMEM((4, 2, 4, 4, 16, 128), BF),
            pltpu.VMEM((4, 2, NZ, 64, 128), BF),
            pltpu.VMEM((4, 2, NZ, 64, 128), BF),
            pltpu.VMEM((NZ, 16, 128), BF),
            pltpu.VMEM((NZ, ROWS, 256), BF),
            pltpu.VMEM((2, NZ, 16, TOK), BF),
            pltpu.VMEM((NY, 256, TOK), F32),
            pltpu.VMEM((NY, 8, TOK), F32),
            pltpu.VMEM((2, NZ, ROWS, 256), BF),
            pltpu.VMEM((2, NZ, 1, 128), F32),
            pltpu.VMEM((2, NZ, ROWS, 256), BF),
            pltpu.VMEM((2, NZ, 1, 128), F32),
            pltpu.VMEM((2, NY, ROWS, 256), BF),
            pltpu.VMEM((2, NY, ROWS, 256), F32),
            pltpu.VMEM((2, NY, ROWS, D), BF),
            pltpu.VMEM((ROWS, D), BF),
            pltpu.VMEM((NZ, ROWS, 256), BF),
            pltpu.SemaphoreType.DMA((N_SEM,)),
            pltpu.SemaphoreType.DMA((N_SEM,)),
            pltpu.SemaphoreType.DMA((8,)),
        ],
        compiler_params=pltpu.CompilerParams(
            collective_id=0, has_side_effects=True, vmem_limit_bytes=63 * 1024 * 1024
        ),
    )(
        cache_len,
        slot_page,
        block_in[0],
        accept,
        cache_kv[0],
        w_query.T,
        w_key_value.T,
        w_out.T,
        w_up.T,
        w_down,
        gain_attn[None],
        gain_mlp[None],
    )
    return result.reshape(1, TOK, D)


def solution(mesh):
    in_specs = (
        P("seq", None, None),
        P(None, "seq", None),
        P("seq"),
        P("seq", "tok"),
        P("seq", "tok", None, None),
        P("seq", "tok"),
        P("seq", "tok"),
        P("seq", "tok"),
        P(),
        P("seq", "tok"),
        P("tok", "seq"),
        P(),
    )
    out_specs = P("seq", None, None)
    return jax.shard_map(shards, mesh=mesh, in_specs=in_specs, out_specs=out_specs, check_vma=False)
```

```python
import jax
import jax.numpy as jnp
from jax import lax
from jax.experimental import pallas as pl
from jax.experimental.pallas import tpu as pltpu
from jax.sharding import PartitionSpec as P

MESH = pl.DeviceIdType.MESH
BF = jnp.bfloat16
F32 = jnp.float32

D = 1024
TOK = 256
NZ, NY, NX = 16, 4, 4
ROWS = TOK // NZ
KEYS = 384
EPSILON = 1e-05
FLOOR_SCORE = -1e30
MASKED = -3e38

(WS, KVZ, OZ, QZ, KVX, OX, QX, KVC, OC, QC, WS2, KPZ, LIM, OY) = range(14)
CY = 14
UP, DOWN = 18, 26
PASS = 34
FAR_FIRST = (8, 7, 9, 6, 10, 5, 11, 4, 12, 3, 13, 2, 14, 1, 15)
(GQZ, RSZ, RSZM, GAY, GOY, RFY) = range(6)
FIN_Y, FIN_Z = PASS + 12, PASS + 12
N_SEM = PASS + 28


def dot_nn(a, b):
    return lax.dot_general(a, b, (((1,), (0,)), ((), ())), preferred_element_type=F32)


def dot_nt(a, b):
    return lax.dot_general(a, b, (((1,), (1,)), ((), ())), preferred_element_type=F32)


def layer_norm(values, gain):
    average = jnp.mean(values, axis=-1, keepdims=True)
    centered = values - average
    variance = jnp.mean(centered * centered, axis=-1, keepdims=True)
    return centered * lax.rsqrt(variance + EPSILON) * gain


def kernel(
    len_ref, page_ref, x_hbm, accept_hbm, cache_ref, wq_ref, wkv_ref, wo_ref, wu_ref, wd_ref, ga_hbm, gm_hbm,
    out_ref,
    x_ref, accept_ref, ga_ref, gm_ref, kvb, vt, lim, ws, ws2, kp, rkp, qw, kvw, ow, up, down,
    hold, qz, qt, po, pm, tz, tzm, rz, rzm, att, ob, fp, fin, fz,
    ssem, rsem, lsem,
):
    s, t = lax.axis_index("seq"), lax.axis_index("tok")
    x, c = lax.div(s, 2), lax.rem(s, 2)
    z, y = lax.div(t, NY), lax.rem(t, NY)
    za, zc = lax.div(z, 8), lax.rem(z, 2)
    to_kv = lax.div(lax.rem(z, 8), 2)
    to_q = lax.div(z, 4)
    to_t = lax.rem(t, NZ) * NY + lax.div(t, NZ)
    from_t = (NY * y + lax.div(z, NY)) * NY + lax.rem(z, NY)
    to_p = (lax.rem(t, 8) + 8 * lax.div(t, 32)) * NY + lax.rem(lax.div(t, 8), 4)
    from_p = 8 * y + z + 24 * za

    def dev_z(k, row=None):
        zp = lax.rem(z + k, NZ)
        return zp, {"seq": s, "tok": zp * NY + (y if row is None else row)}

    def dev_y(k):
        yp = lax.rem(y + k, NY)
        return yp, {"seq": s, "tok": z * NY + yp}

    def dev_s(k, tok):
        return {"seq": lax.rem(s + k, 2 * NX), "tok": tok}

    def dev_x(k):
        return {"seq": lax.rem(x + k, NX) * 2 + c, "tok": t}

    ow_own = ow.at[:, :, y]
    partner = {"seq": x * 2 + 1 - c, "tok": t}

    def put(src, dst, ph, dev, rph=None):
        return pltpu.make_async_remote_copy(
            src_ref=src,
            dst_ref=dst,
            send_sem=ssem.at[ph],
            recv_sem=rsem.at[ph if rph is None else rph],
            device_id=dev,
            device_id_type=MESH,
        )

    def arrived(view, ph):
        put(view, view, ph, partner).wait_recv()

    def sent(view, ph):
        put(view, view, ph, partner).wait_send()

    def here(src, dst, ph):
        pltpu.make_async_copy(src, dst, rsem.at[ph]).start()

    def tell(dev):
        pl.semaphore_signal(barrier, inc=1, device_id=dev, device_id_type=MESH)

    def lanes(start, size):
        return pl.ds(pl.multiple_of(start, size), size)

    barrier = pltpu.get_barrier_semaphore()
    for k in range(8):
        @pl.when((k > 0) | (from_t != t))
        def _():
            tell(dev_s(k, from_t))

        @pl.when((k > 0) | (from_p != t))
        def _():
            tell(dev_s(k, from_p))
    for k in range(1, NX):
        tell(dev_x(k))
    tell(partner)
    for k in range(1, NY):
        tell(dev_y(k)[1])

    @pl.loop(1, NZ)
    def _(k):
        tell(dev_z(k)[1])

    @pl.loop(0, NZ)
    def _(i):
        zs, ys = 8 * lax.div(i, 8) + 2 * y + lax.rem(lax.div(i, 4), 2), lax.rem(i, 4)

        @pl.when((zs != z) | (ys != y))
        def _():
            tell({"seq": s, "tok": zs * NY + ys})

    @pl.loop(0, NZ)
    def _(i):
        zs, ys = 4 * y + lax.div(i, 4), lax.rem(i, 4)

        @pl.when((zs != z) | (ys != y))
        def _():
            tell({"seq": s, "tok": zs * NY + ys})

    local = [
        pltpu.make_async_copy(a, b, lsem.at[i])
        for i, (a, b) in enumerate(
            (
                (x_hbm, x_ref),
                (cache_ref.at[:, :, lanes(y * 256, 256)], kvb.at[y, 0]),
                (cache_ref.at[:, :, lanes(D + y * 256, 256)], kvb.at[y, 1]),
                (wu_ref, up.at[x, c, z]),
                (wd_ref, down.at[x, c, z]),
                (accept_hbm, accept_ref),
                (ga_hbm, ga_ref),
                (gm_hbm, gm_ref),
            )
        )
    ]
    for copy in local:
        copy.start()

    others = (to_t != t).astype(jnp.int32) + (to_kv != y).astype(jnp.int32) + (to_q != y).astype(jnp.int32)
    others += (to_p != t).astype(jnp.int32)
    pl.semaphore_wait(barrier, 14 + NX + (NY - 1) + 3 * (NZ - 1) + others)

    for k in range(8):
        @pl.when((k > 0) | (to_t != t))
        def _():
            put(wq_ref, ws.at[s], WS, dev_s(k, to_t)).start()

        @pl.when((k > 0) | (to_p != t))
        def _():
            put(wkv_ref, ws2.at[s], WS2, dev_s(k, to_p)).start()

    @pl.when(to_t == t)
    def _():
        here(wq_ref, ws.at[s], WS)

    @pl.when(to_p == t)
    def _():
        here(wkv_ref, ws2.at[s], WS2)

    for k in (1, 3, 2):
        yp, dev = dev_y(k)
        put(cache_ref.at[:, :, lanes(yp * 256, 256)], kvb.at[y, 0], CY + k, dev).start()
        put(cache_ref.at[:, :, lanes(D + yp * 256, 256)], kvb.at[y, 1], CY + k, dev).start()
    length = len_ref[0].astype(F32)
    slot_row = lax.broadcasted_iota(jnp.int32, (8, 128), 0)
    limits = jnp.zeros((8, 128), F32)
    for j in range(3):
        page = page_ref[0, j].astype(F32)
        limits = jnp.where(slot_row == j, jnp.where(page >= 0, length - page * 128, 0.0), limits)
    lim[y] = limits
    for k in range(1, NY):
        put(lim.at[y], lim.at[y], LIM, dev_y(k)[1]).start()

    def spread(src, dst, ph, row):
        @pl.loop(1, NZ)
        def _(k):
            put(src, dst, ph, dev_z(k, row)[1]).start()

        @pl.when(row != y)
        def _():
            put(src, dst, ph, dev_z(0, row)[1]).start()

        @pl.when(row == y)
        def _():
            here(src, dst, ph)

    def direct(src, ref, ph):
        for k in (4, 12, 3, 13, 2, 14, 1, 15):
            landed = ph + {4: 1, 12: 2}.get(k, 0)
            put(src, ref.at[x, c, z], ph, dev_z(k)[1], landed).start()

    def relay(ref, ph):
        left, right = lax.rem(z + 12, NZ), lax.rem(z + 4, NZ)
        arrived(ref.at[x, c, left], ph + 1)
        for k in (4, 3, 2, 1):
            put(ref.at[x, c, left], ref.at[x, c, left], ph + 3, dev_z(k)[1]).start()
        arrived(ref.at[x, c, right], ph + 2)
        for k in (13, 14, 15):
            put(ref.at[x, c, right], ref.at[x, c, right], ph + 3, dev_z(k)[1]).start()

    def part(n):
        return (0, 9) if n == 0 else (9, 16)

    def to_x(ref, ph):
        for k in (2, 1, 3):
            put(ref.at[x, c], ref.at[x, c], ph, dev_x(k)).start()

    def ff_to_x(ref, ph, n):
        if n == 0:
            arrived(ref.at[0, 0, pl.ds(0, 6)], ph)
        else:
            arrived(ref.at[0, 0, pl.ds(0, 7)], ph + 3)

        @pl.loop(*part(n))
        def _(i):
            slot = lax.rem(z + 12 + i, NZ)
            for k in (2, 1, 3):
                put(ref.at[x, c, slot], ref.at[x, c, slot], ph + 4 + n, dev_x(k)).start()

    def ff_to_core(ref, ph, n):
        low, high = part(n)
        arrived(ref.at[pl.ds(0, 3), 0, pl.ds(0, high - low)], ph + 4 + n)

        @pl.loop(low, high)
        def _(i):
            slot = lax.rem(z + 12 + i, NZ)
            put(ref.at[:, c, slot], ref.at[:, c, slot], ph + 6 + n, partner).start()

    def ff_ready(ref, ph):
        for n in range(2):
            low, high = part(n)
            arrived(ref.at[:, 0, pl.ds(0, high - low)], ph + 6 + n)

    def to_core(ref, xs, cs):
        arrived(ref.at[pl.ds(0, 3), 0], xs)
        put(ref.at[:, c], ref.at[:, c], cs, partner).start()

    spread(wo_ref, ow.at[x, c, to_q, lax.rem(z, 4), y], OZ, to_q)
    direct(wu_ref, up, UP)
    arrived(ws, WS)
    local[0].wait()
    wq_cols = jnp.concatenate([ws[i] for i in range(8)], axis=1)
    qt[0, z] = dot_nt(wq_cols, x_ref[...]).astype(BF) * jnp.asarray(0.125, BF)

    for k in FAR_FIRST:
        put(qt.at[0, z], qt.at[0, z], PASS + GQZ, dev_z(k)[1]).start()
    arrived(ws2, WS2)
    kv_cols = jnp.concatenate([ws2[i] for i in range(8)], axis=1)
    kv_cols = jnp.concatenate([kv_cols, jnp.zeros((96, D), BF)], axis=0)
    kp[...] = dot_nt(x_ref[...], kv_cols).astype(BF).reshape(NZ, ROWS, 128)
    for k in FAR_FIRST:
        zp, dev = dev_z(k)
        put(kp.at[zp], rkp.at[z], KPZ, dev).start()
    rkp[z] = kp[z]
    direct(wd_ref, down, DOWN)

    vt[:, :, 128:144, :] = jnp.ones((NY, 2, 16, KEYS), BF)

    def turn(j):
        for i in range(2):
            for n in range(3):
                vt[j, i, 0:128, 128 * n : 128 * (n + 1)] = jnp.transpose(kvb[j, 1, n, :, 128 * i : 128 * i + 128])

    local[1].wait()
    local[2].wait()
    turn(y)
    arrived(ow.at[0, 0, 0], OZ)
    to_x(ow_own, OX)
    local[3].wait()
    local[4].wait()
    for k in (1, 3, 2):
        src = lax.rem(y + NY - k, NY)
        arrived(kvb.at[src], CY + k)
        turn(src)
    arrived(lim.at[pl.ds(0, 3)], LIM)
    for i in range(5, 8):
        local[i].wait()

    own_rows = pl.ds(pl.multiple_of(z * ROWS, ROWS), ROWS)
    current = x_ref[own_rows, :]

    for p in range(2):
        base = PASS + 6 * p
        if p == 1:
            for k in range(1, NY):
                put(ow_own, ow_own, OY, dev_y(k)[1]).start()
            w_q = jnp.concatenate([qw[i, j].reshape(256, 128) for i in range(4) for j in range(2)], axis=1)
            qz[z] = dot_nt(current, w_q).astype(BF) * jnp.asarray(0.125, BF)

            for k in FAR_FIRST:
                put(qz.at[z], qz.at[z], base + GQZ, dev_z(k)[1]).start()
            arrived(qz.at[pl.ds(0, NZ - 1)], base + GQZ)
            to_core(kvw, KVX, KVC)
            qt[1] = jnp.transpose(qz[...].reshape(TOK, 256)).reshape(NZ, 16, TOK)
        else:
            arrived(qt.at[p, pl.ds(0, NZ - 1)], base + GQZ)
            relay(up, UP)
            ff_to_x(up, UP, 0)
            spread(wq_ref, qw.at[x, c, lax.rem(z, 4), y], QZ, to_q)

        @pl.loop(0, NY)
        def _(j):
            if p == 0:
                @pl.when(j == 1)
                def _():
                    relay(down, DOWN)
                    ff_to_x(down, DOWN, 0)

            for i in range(2):
                keys = kvb[j, 0, :, :, 128 * i : 128 * i + 128].reshape(KEYS, 128)
                q_pair = qt[p, 8 * i : 8 * i + 8].reshape(2, 64, TOK)
                none = jnp.zeros((64, TOK), BF)
                both = jnp.concatenate(
                    [
                        jnp.concatenate([q_pair[0], none], axis=1),
                        jnp.concatenate([none, q_pair[1]], axis=1),
                    ],
                    axis=0,
                )
                scores = dot_nn(keys, both)
                offsets = lax.broadcasted_iota(jnp.int32, (128, 2 * TOK), 0).astype(F32)
                masked = jnp.concatenate(
                    [
                        jnp.where(
                            offsets < jnp.concatenate([lim[j, n : n + 1, :]] * 4, axis=1),
                            scores[128 * n : 128 * (n + 1)],
                            MASKED,
                        )
                        for n in range(3)
                    ],
                    axis=0,
                )
                peaks = jnp.maximum(jnp.max(masked, axis=0, keepdims=True), FLOOR_SCORE)
                weights = jnp.exp(masked - peaks).astype(BF)
                summed = dot_nn(vt[j, i], weights)
                po[j, 128 * i : 128 * i + 64, :] = summed[0:64, 0:TOK]
                po[j, 128 * i + 64 : 128 * i + 128, :] = summed[64:128, TOK : 2 * TOK]
                pm[j, 2 * i : 2 * i + 1, :] = peaks[:, 0:TOK]
                pm[j, 2 * i + 1 : 2 * i + 2, :] = peaks[:, TOK : 2 * TOK]
                pm[j, 4 + 2 * i : 5 + 2 * i, :] = summed[128:129, 0:TOK]
                pm[j, 5 + 2 * i : 6 + 2 * i, :] = summed[128:129, TOK : 2 * TOK]

        if p == 0:
            arrived(rkp.at[pl.ds(0, NZ - 1)], KPZ)
            pieces = [
                sum(pltpu.roll(rkp[4 * i + n].astype(F32), 32 * n, 1) for n in range(1, 4)) + rkp[4 * i].astype(F32)
                for i in range(4)
            ]
            pair = jnp.concatenate(pieces, axis=1)
        else:
            arrived(kvw.at[:, 0], KVC)
            w_pair = jnp.concatenate([kvw[i, j].reshape(512, 128) for i in range(4) for j in range(2)], axis=1)
            pair = dot_nt(current, w_pair)
        row_head = lax.div(lax.broadcasted_iota(jnp.int32, (64, 256), 0), 16)
        lane_head = lax.div(lax.broadcasted_iota(jnp.int32, (64, 256), 1), 64)
        own_head = row_head == lane_head
        k_block = jnp.where(own_head, jnp.concatenate([pair[:, 0:256]] * 4, axis=0), 0.0).astype(BF)
        v_block = jnp.where(own_head, jnp.concatenate([pair[:, 256:512]] * 4, axis=0), 0.0)
        b_scores = dot_nn(k_block, qt[p].reshape(256, TOK)).reshape(4, 16, TOK)
        b_peak = jnp.max(b_scores, axis=1)
        b_weights = jnp.exp(b_scores - b_peak[:, None, :]).astype(BF)
        b_total = jnp.sum(b_weights.astype(F32), axis=1)
        b_sum = dot_nn(jnp.transpose(v_block).astype(BF), b_weights.reshape(64, TOK))

        peaks_y = pm[:, 0:4, :]
        peak = jnp.maximum(jnp.max(peaks_y, axis=0), b_peak)
        scale = jnp.exp(peaks_y - peak[None])
        b_scale = jnp.exp(b_peak - peak)
        total = jnp.sum(scale * pm[:, 4:8, :], axis=0) + b_scale * b_total
        parts = []
        for h in range(4):
            rows = slice(64 * h, 64 * h + 64)
            value = b_sum[rows] * b_scale[h : h + 1]
            for i in range(NY):
                value += po[i, rows, :] * scale[i, h : h + 1]
            parts.append(value)
        tz[p] = jnp.transpose(jnp.concatenate(parts, axis=0)).astype(BF).reshape(NZ, ROWS, 256)
        both = jnp.concatenate([peak, total], axis=0)
        belongs = lax.broadcasted_iota(jnp.int32, (8, 128), 0) == lax.div(
            lax.broadcasted_iota(jnp.int32, (8, 128), 1), ROWS
        )
        steps = [pltpu.roll(both[:, 128 * i : 128 * i + 128], 0, 1, stride=ROWS, stride_axis=0) for i in range(2)]
        for i in range(NZ):
            moved = pltpu.roll(steps[i // 8], (128 - ROWS * (i % 8)) % 128, 1)
            tzm[p, i] = jnp.sum(jnp.where(belongs, moved, 0.0), axis=0, keepdims=True)

        for k in FAR_FIRST:
            zp, dev = dev_z(k)
            put(tzm.at[p, zp], rzm.at[p, z], base + RSZM, dev).start()
            put(tz.at[p, zp], rz.at[p, z], base + RSZ, dev).start()

        rz[p, z] = tz[p, z]
        rzm[p, z] = tzm[p, z]
        if p == 0:
            ff_to_x(up, UP, 1)
            ff_to_x(down, DOWN, 1)
            ff_to_core(up, UP, 0)
            ff_to_core(down, DOWN, 0)

        arrived(rzm.at[p, pl.ds(0, NZ - 1)], base + RSZM)
        stats = rzm[p].reshape(NZ, 128)
        scale_z = jnp.exp(stats - jnp.max(stats, axis=0, keepdims=True))
        share = scale_z / jnp.sum(scale_z * pltpu.roll(stats, 64, 1), axis=0, keepdims=True)
        share = jnp.transpose(jnp.concatenate([share, jnp.zeros((128 - NZ, 128), F32)], axis=0))
        arrived(rz.at[p, pl.ds(0, NZ - 1)], base + RSZ)
        if p == 0:
            spread(wkv_ref, kvw.at[x, c, za, zc, y], KVZ, to_kv)
            to_core(ow_own, OX, OC)
        lower = lax.broadcasted_iota(jnp.int32, (ROWS, 128), 1) < 64
        halves = [jnp.zeros((ROWS, 128), F32), jnp.zeros((ROWS, 128), F32)]
        for i in range(NZ):
            for n in range(2):
                low = jnp.broadcast_to(share[32 * n : 32 * n + 16, i : i + 1], (ROWS, 128))
                high = jnp.broadcast_to(share[32 * n + 16 : 32 * n + 32, i : i + 1], (ROWS, 128))
                halves[n] += jnp.where(lower, low, high) * rz[p, i, :, 128 * n : 128 * n + 128].astype(F32)
        att[p, y] = jnp.concatenate(halves, axis=1).astype(BF)
        for k in range(1, NY):
            put(att.at[p, y], att.at[p, y], base + GAY, dev_y(k)[1]).start()
        if p == 0:
            ff_to_core(up, UP, 1)
            arrived(ow.at[:, 0, 0], OC)
        arrived(att.at[p, pl.ds(0, 3)], base + GAY)

        heads = jnp.concatenate([att[p, i] for i in range(NY)], axis=1)
        if p == 0:
            w_o = jnp.concatenate([ow[i, j, y].reshape(256, 128) for i in range(4) for j in range(2)], axis=1)
            ob[y] = dot_nt(heads, w_o)
            for k in range(1, NY):
                put(ob.at[y], ob.at[y], base + GOY, dev_y(k)[1]).start()
            ff_to_core(down, DOWN, 1)
            arrived(qw.at[0, 0], QZ)
            to_x(qw, QX)
            arrived(ob.at[pl.ds(0, 3)], base + GOY)
            projected = jnp.concatenate([ob[i] for i in range(NY)], axis=1)
        else:
            arrived(ow.at[:, :, pl.ds(0, 3)], OY)
            w_o = jnp.concatenate([ow[i, j].reshape(D, 128) for i in range(4) for j in range(2)], axis=1)
            projected = dot_nt(heads, w_o)
        settled = layer_norm(current.astype(F32) + projected, ga_ref[...]).astype(BF)

        if p == 0:
            ff_ready(up, UP)
        w_u = jnp.concatenate([up[i, j].reshape(D, 128) for i in range(4) for j in range(2)], axis=1)
        product = dot_nt(settled, w_u)
        hidden = (0.5 * product * (1.0 + lax.erf(product * (0.5**0.5)))).astype(BF)
        if p == 0:
            ff_ready(down, DOWN)
        w_d = jnp.concatenate([down[i, j].reshape(D, 128) for i in range(4) for j in range(2)], axis=1)
        fp[p, y] = dot_nn(hidden, w_d).astype(BF)
        for k in range(1, NY):
            put(fp.at[p, y], fp.at[p, y], base + RFY, dev_y(k)[1]).start()
        if p == 0:
            to_core(qw, QX, QC)
            arrived(kvw.at[0, 0], KVZ)
            to_x(kvw, KVX)
            arrived(qw.at[:, 0], QC)
        arrived(fp.at[p, pl.ds(0, 3)], base + RFY)
        projected = fp[p, 0].astype(F32) + fp[p, 1].astype(F32) + fp[p, 2].astype(F32) + fp[p, 3].astype(F32)
        finished = layer_norm(settled.astype(F32) + projected, gm_ref[...])
        own_token = lax.broadcasted_iota(jnp.int32, (ROWS, TOK), 1) == z * ROWS + lax.broadcasted_iota(
            jnp.int32, (ROWS, TOK), 0
        )
        taken = jnp.sum(jnp.where(own_token, accept_ref[p].astype(F32), 0.0), axis=1, keepdims=True) > 0.5
        current = jnp.where(taken, finished, current.astype(F32)).astype(BF)

    fin[...] = current
    quarter = lanes(y * 256, 256)
    fz[z] = fin[:, quarter]

    def hand_on(zp):
        for k in range(1, NY):
            put(fz.at[zp], out_ref.at[zp, :, quarter], FIN_Y, dev_y(k)[1]).start()

    def in_turn(i):
        near = lax.div(i, 2) + 1
        return jnp.where(lax.rem(i, 2) == 0, near, NZ - near)

    @pl.loop(0, NZ - 1)
    def _(i):
        k = in_turn(i)
        put(fz.at[z], fz.at[z], FIN_Z + k, dev_z(k)[1]).start()

    hand_on(z)

    @pl.loop(0, NZ - 1)
    def _(i):
        k = in_turn(i)
        zp = lax.rem(z + NZ - k, NZ)
        arrived(fz.at[zp], FIN_Z + k)
        hand_on(zp)

    out_ref[:, :, quarter] = fz[...]
    arrived(out_ref.at[:, :, pl.ds(0, 768)], FIN_Y)

    def sent_but_own(ref, axis_end, ph, own):
        @pl.when(own)
        def _():
            sent(ref.at[pl.ds(0, axis_end - 1)], ph)

        @pl.when(jnp.logical_not(own))
        def _():
            sent(ref.at[pl.ds(0, axis_end)], ph)

    sent_but_own(ws, 8, WS, to_t == t)
    sent_but_own(qz, NZ, KVZ, to_kv == y)
    sent_but_own(hold, NZ, OZ, to_q == y)
    sent_but_own(hold, NZ, QZ, to_q == y)
    sent_but_own(ws2, 8, WS2, to_p == t)
    sent(rkp.at[pl.ds(0, NZ - 1)], KPZ)
    sent(ow.at[:, :, pl.ds(0, 3)], OY)
    for ref, xs, cs in ((qw, QX, QC), (kvw, KVX, KVC), (ow_own, OX, OC)):
        sent(ref.at[pl.ds(0, 3), 0], xs)
        sent(ref.at[:, 0], cs)
    for ph in (UP, DOWN):
        sent(up.at[0, 0, pl.ds(0, 8)], ph)
        sent(up.at[0, 0, pl.ds(0, 7)], ph + 3)
        for n in range(2):
            low, high = part(n)
            sent(up.at[pl.ds(0, 3), 0, pl.ds(0, high - low)], ph + 4 + n)
            sent(up.at[:, 0, pl.ds(0, high - low)], ph + 6 + n)
    for k in range(1, NY):
        sent(kvb.at[0], CY + k)
    sent(lim.at[pl.ds(0, 3)], LIM)
    for p in range(2):
        base = PASS + 6 * p
        sent(qz.at[pl.ds(0, NZ - 1)], base + GQZ)
        sent(rz.at[p, pl.ds(0, NZ - 1)], base + RSZ)
        sent(rzm.at[p, pl.ds(0, NZ - 1)], base + RSZM)
        sent(att.at[p, pl.ds(0, 3)], base + GAY)
        if p == 0:
            sent(ob.at[pl.ds(0, 3)], base + GOY)
        sent(fp.at[p, pl.ds(0, 3)], base + RFY)

    @pl.loop(1, NZ)
    def _(k):
        sent(fz.at[0], FIN_Z + k)

    sent(out_ref.at[:, :, pl.ds(0, 768)], FIN_Y)


def shards(
    block_in, accept, cache_len, slot_page, cache_kv, w_query, w_key_value, w_out, gain_attn, w_up, w_down, gain_mlp
):
    smem = pl.BlockSpec(memory_space=pltpu.SMEM)
    result = pl.pallas_call(
        kernel,
        out_shape=jax.ShapeDtypeStruct((NZ, ROWS, D), BF),
        in_specs=[smem, smem] + [pl.BlockSpec(memory_space=pltpu.HBM)] * 10,
        out_specs=pl.BlockSpec(memory_space=pltpu.VMEM),
        scratch_shapes=[
            pltpu.VMEM((TOK, D), BF),
            pltpu.VMEM((2, 1, TOK), jnp.int32),
            pltpu.VMEM((1, D), F32),
            pltpu.VMEM((1, D), F32),
            pltpu.VMEM((NY, 2, 3, 128, 256), BF),
            pltpu.VMEM((NY, 2, 144, KEYS), BF),
            pltpu.VMEM((NY, 8, 128), F32),
            pltpu.VMEM((8, 16, 128), BF),
            pltpu.VMEM((8, 32, 128), BF),
            pltpu.VMEM((NZ, ROWS, 128), BF),
            pltpu.VMEM((NZ, ROWS, 128), BF),
            pltpu.VMEM((4, 2, 4, 4, 16, 128), BF),
            pltpu.VMEM((4, 2, 2, 2, 4, 32, 128), BF),
            pltpu.VMEM((4, 2, NY, 4, 4, 16, 128), BF),
            pltpu.VMEM((4, 2, NZ, 64, 128), BF),
            pltpu.VMEM((4, 2, NZ, 64, 128), BF),
            pltpu.VMEM((NZ, 16, 128), BF),
            pltpu.VMEM((NZ, ROWS, 256), BF),
            pltpu.VMEM((2, NZ, 16, TOK), BF),
            pltpu.VMEM((NY, 256, TOK), F32),
            pltpu.VMEM((NY, 8, TOK), F32),
            pltpu.VMEM((2, NZ, ROWS, 256), BF),
            pltpu.VMEM((2, NZ, 1, 128), F32),
            pltpu.VMEM((2, NZ, ROWS, 256), BF),
            pltpu.VMEM((2, NZ, 1, 128), F32),
            pltpu.VMEM((2, NY, ROWS, 256), BF),
            pltpu.VMEM((NY, ROWS, 256), F32),
            pltpu.VMEM((2, NY, ROWS, D), BF),
            pltpu.VMEM((ROWS, D), BF),
            pltpu.VMEM((NZ, ROWS, 256), BF),
            pltpu.SemaphoreType.DMA((N_SEM,)),
            pltpu.SemaphoreType.DMA((N_SEM,)),
            pltpu.SemaphoreType.DMA((8,)),
        ],
        compiler_params=pltpu.CompilerParams(
            collective_id=0, has_side_effects=True, vmem_limit_bytes=63 * 1024 * 1024
        ),
    )(
        cache_len,
        slot_page,
        block_in[0],
        accept,
        cache_kv[0],
        w_query.T,
        w_key_value.T,
        w_out.T,
        w_up.T,
        w_down,
        gain_attn[None],
        gain_mlp[None],
    )
    return result.reshape(1, TOK, D)


def solution(mesh):
    in_specs = (
        P("seq", None, None),
        P(None, "seq", None),
        P("seq"),
        P("seq", "tok"),
        P("seq", "tok", None, None),
        P("seq", "tok"),
        P("seq", "tok"),
        P("seq", "tok"),
        P(),
        P("seq", "tok"),
        P("tok", "seq"),
        P(),
    )
    out_specs = P("seq", None, None)
    return jax.shard_map(shards, mesh=mesh, in_specs=in_specs, out_specs=out_specs, check_vma=False)
```

```python
import jax
import jax.numpy as jnp
from jax import lax
from jax.experimental import pallas as pl
from jax.experimental.pallas import tpu as pltpu
from jax.sharding import PartitionSpec as P

MESH = pl.DeviceIdType.MESH
BF = jnp.bfloat16
F32 = jnp.float32

D = 1024
TOK = 256
NZ, NY, NX = 16, 4, 4
ROWS = TOK // NZ
KEYS = 384
EPSILON = 1e-05
FLOOR_SCORE = -1e30
MASKED = -3e38

(WS, KVZ, OZ, QZ, KVX, OX, QX, KVC, OC, QC, WS2, KPZ, LIM, OY) = range(14)
CY = 14
UP, DOWN = 18, 26
PASS = 34
FAR_FIRST = (8, 7, 9, 6, 10, 5, 11, 4, 12, 3, 13, 2, 14, 1, 15)
(GQZ, RSZ, RSZM, GAY, GOY, RFY) = range(6)
FIN_Y, FIN_Z = PASS + 12, PASS + 12
N_SEM = PASS + 28


def dot_nn(a, b):
    return lax.dot_general(a, b, (((1,), (0,)), ((), ())), preferred_element_type=F32)


def dot_nt(a, b):
    return lax.dot_general(a, b, (((1,), (1,)), ((), ())), preferred_element_type=F32)


def layer_norm(values, gain):
    average = jnp.mean(values, axis=-1, keepdims=True)
    centered = values - average
    variance = jnp.mean(centered * centered, axis=-1, keepdims=True)
    return centered * lax.rsqrt(variance + EPSILON) * gain


def kernel(
    len_ref, page_ref, x_hbm, accept_hbm, cache_ref, wq_ref, wkv_ref, wo_ref, wu_ref, wd_ref, ga_hbm, gm_hbm,
    out_ref,
    x_ref, accept_ref, ga_ref, gm_ref, kvb, vt, lim, ws, ws2, kp, rkp, qw, kvw, ow, up, down,
    hold, qz, qt, po, pm, tz, tzm, rz, rzm, att, ob, fp, fin, fz,
    ssem, rsem, lsem,
):
    s, t = lax.axis_index("seq"), lax.axis_index("tok")
    x, c = lax.div(s, 2), lax.rem(s, 2)
    z, y = lax.div(t, NY), lax.rem(t, NY)
    za, zc = lax.div(z, 8), lax.rem(z, 2)
    to_kv = lax.div(lax.rem(z, 8), 2)
    to_q = lax.div(z, 4)
    to_t = lax.rem(t, NZ) * NY + lax.div(t, NZ)
    from_t = (NY * y + lax.div(z, NY)) * NY + lax.rem(z, NY)
    to_p = (lax.rem(t, 8) + 8 * lax.div(t, 32)) * NY + lax.rem(lax.div(t, 8), 4)
    from_p = 8 * y + z + 24 * za

    def dev_z(k, row=None):
        zp = lax.rem(z + k, NZ)
        return zp, {"seq": s, "tok": zp * NY + (y if row is None else row)}

    def dev_y(k):
        yp = lax.rem(y + k, NY)
        return yp, {"seq": s, "tok": z * NY + yp}

    def dev_s(k, tok):
        return {"seq": lax.rem(s + k, 2 * NX), "tok": tok}

    def dev_x(k):
        return {"seq": lax.rem(x + k, NX) * 2 + c, "tok": t}

    ow_own = ow.at[:, :, y]
    partner = {"seq": x * 2 + 1 - c, "tok": t}

    def put(src, dst, ph, dev, rph=None):
        return pltpu.make_async_remote_copy(
            src_ref=src,
            dst_ref=dst,
            send_sem=ssem.at[ph],
            recv_sem=rsem.at[ph if rph is None else rph],
            device_id=dev,
            device_id_type=MESH,
        )

    def arrived(view, ph):
        put(view, view, ph, partner).wait_recv()

    def sent(view, ph):
        put(view, view, ph, partner).wait_send()

    def here(src, dst, ph):
        pltpu.make_async_copy(src, dst, rsem.at[ph]).start()

    def tell(dev):
        pl.semaphore_signal(barrier, inc=1, device_id=dev, device_id_type=MESH)

    def lanes(start, size):
        return pl.ds(pl.multiple_of(start, size), size)

    barrier = pltpu.get_barrier_semaphore()
    for k in range(8):
        @pl.when((k > 0) | (from_t != t))
        def _():
            tell(dev_s(k, from_t))

        @pl.when((k > 0) | (from_p != t))
        def _():
            tell(dev_s(k, from_p))
    for k in range(1, NX):
        tell(dev_x(k))
    tell(partner)
    for k in range(1, NY):
        tell(dev_y(k)[1])

    @pl.loop(1, NZ)
    def _(k):
        tell(dev_z(k)[1])

    @pl.loop(0, NZ)
    def _(i):
        zs, ys = 8 * lax.div(i, 8) + 2 * y + lax.rem(lax.div(i, 4), 2), lax.rem(i, 4)

        @pl.when((zs != z) | (ys != y))
        def _():
            tell({"seq": s, "tok": zs * NY + ys})

    @pl.loop(0, NZ)
    def _(i):
        zs, ys = 4 * y + lax.div(i, 4), lax.rem(i, 4)

        @pl.when((zs != z) | (ys != y))
        def _():
            tell({"seq": s, "tok": zs * NY + ys})

    local = [
        pltpu.make_async_copy(a, b, lsem.at[i])
        for i, (a, b) in enumerate(
            (
                (x_hbm, x_ref),
                (cache_ref.at[:, :, lanes(y * 256, 256)], kvb.at[y, 0]),
                (cache_ref.at[:, :, lanes(D + y * 256, 256)], kvb.at[y, 1]),
                (wu_ref, up.at[x, c, z]),
                (wd_ref, down.at[x, c, z]),
                (accept_hbm, accept_ref),
                (ga_hbm, ga_ref),
                (gm_hbm, gm_ref),
            )
        )
    ]
    for copy in local:
        copy.start()

    others = (to_t != t).astype(jnp.int32) + (to_kv != y).astype(jnp.int32) + (to_q != y).astype(jnp.int32)
    others += (to_p != t).astype(jnp.int32)
    pl.semaphore_wait(barrier, 14 + NX + (NY - 1) + 3 * (NZ - 1) + others)

    for k in range(8):
        @pl.when((k > 0) | (to_t != t))
        def _():
            put(wq_ref, ws.at[s], WS, dev_s(k, to_t)).start()

        @pl.when((k > 0) | (to_p != t))
        def _():
            put(wkv_ref, ws2.at[s], WS2, dev_s(k, to_p)).start()

    @pl.when(to_t == t)
    def _():
        here(wq_ref, ws.at[s], WS)

    @pl.when(to_p == t)
    def _():
        here(wkv_ref, ws2.at[s], WS2)

    for k in (1, 3, 2):
        yp, dev = dev_y(k)
        put(cache_ref.at[:, :, lanes(yp * 256, 256)], kvb.at[y, 0], CY + k, dev).start()
        put(cache_ref.at[:, :, lanes(D + yp * 256, 256)], kvb.at[y, 1], CY + k, dev).start()
    length = len_ref[0].astype(F32)
    slot_row = lax.broadcasted_iota(jnp.int32, (8, 128), 0)
    limits = jnp.zeros((8, 128), F32)
    for j in range(3):
        page = page_ref[0, j].astype(F32)
        limits = jnp.where(slot_row == j, jnp.where(page >= 0, length - page * 128, 0.0), limits)
    lim[y] = limits
    for k in range(1, NY):
        put(lim.at[y], lim.at[y], LIM, dev_y(k)[1]).start()

    def spread(src, dst, ph, row):
        @pl.loop(1, NZ)
        def _(k):
            put(src, dst, ph, dev_z(k, row)[1]).start()

        @pl.when(row != y)
        def _():
            put(src, dst, ph, dev_z(0, row)[1]).start()

        @pl.when(row == y)
        def _():
            here(src, dst, ph)

    def direct(src, ref, ph):
        for k in (4, 12, 3, 13, 2, 14, 1, 15):
            landed = ph + {4: 1, 12: 2}.get(k, 0)
            put(src, ref.at[x, c, z], ph, dev_z(k)[1], landed).start()

    def relay(ref, ph):
        left, right = lax.rem(z + 12, NZ), lax.rem(z + 4, NZ)
        arrived(ref.at[x, c, left], ph + 1)
        for k in (4, 3, 2, 1):
            put(ref.at[x, c, left], ref.at[x, c, left], ph + 3, dev_z(k)[1]).start()
        arrived(ref.at[x, c, right], ph + 2)
        for k in (13, 14, 15):
            put(ref.at[x, c, right], ref.at[x, c, right], ph + 3, dev_z(k)[1]).start()

    def part(n):
        return (0, 9) if n == 0 else (9, 16)

    def to_x(ref, ph):
        for k in (2, 1, 3):
            put(ref.at[x, c], ref.at[x, c], ph, dev_x(k)).start()

    def ff_to_x(ref, ph, n):
        if n == 0:
            arrived(ref.at[0, 0, pl.ds(0, 6)], ph)
        else:
            arrived(ref.at[0, 0, pl.ds(0, 7)], ph + 3)

        @pl.loop(*part(n))
        def _(i):
            slot = lax.rem(z + 12 + i, NZ)
            for k in (2, 1, 3):
                put(ref.at[x, c, slot], ref.at[x, c, slot], ph + 4 + n, dev_x(k)).start()

    def ff_to_core(ref, ph, n):
        low, high = part(n)
        arrived(ref.at[pl.ds(0, 3), 0, pl.ds(0, high - low)], ph + 4 + n)

        @pl.loop(low, high)
        def _(i):
            slot = lax.rem(z + 12 + i, NZ)
            put(ref.at[:, c, slot], ref.at[:, c, slot], ph + 6 + n, partner).start()

    def ff_ready(ref, ph):
        for n in range(2):
            low, high = part(n)
            arrived(ref.at[:, 0, pl.ds(0, high - low)], ph + 6 + n)

    def to_core(ref, xs, cs):
        arrived(ref.at[pl.ds(0, 3), 0], xs)
        put(ref.at[:, c], ref.at[:, c], cs, partner).start()

    spread(wo_ref, ow.at[x, c, to_q, lax.rem(z, 4), y], OZ, to_q)
    direct(wu_ref, up, UP)
    arrived(ws, WS)
    local[0].wait()
    wq_cols = jnp.concatenate([ws[i] for i in range(8)], axis=1)
    qt[0, z] = dot_nt(wq_cols, x_ref[...]).astype(BF) * jnp.asarray(0.125, BF)

    for k in FAR_FIRST:
        put(qt.at[0, z], qt.at[0, z], PASS + GQZ, dev_z(k)[1]).start()
    arrived(ws2, WS2)
    kv_cols = jnp.concatenate([ws2[i] for i in range(8)], axis=1)
    kv_cols = jnp.concatenate([kv_cols, jnp.zeros((96, D), BF)], axis=0)
    kp[...] = dot_nt(x_ref[...], kv_cols).astype(BF).reshape(NZ, ROWS, 128)
    for k in FAR_FIRST:
        zp, dev = dev_z(k)
        put(kp.at[zp], rkp.at[z], KPZ, dev).start()
    rkp[z] = kp[z]
    direct(wd_ref, down, DOWN)

    vt[:, :, 128:144, :] = jnp.ones((NY, 2, 16, KEYS), BF)

    def turn(j):
        for i in range(2):
            for n in range(3):
                vt[j, i, 0:128, 128 * n : 128 * (n + 1)] = jnp.transpose(kvb[j, 1, n, :, 128 * i : 128 * i + 128])

    local[1].wait()
    local[2].wait()
    turn(y)
    arrived(ow.at[0, 0, 0], OZ)
    to_x(ow_own, OX)
    local[3].wait()
    local[4].wait()
    for k in (1, 3, 2):
        src = lax.rem(y + NY - k, NY)
        arrived(kvb.at[src], CY + k)
        turn(src)
    arrived(lim.at[pl.ds(0, 3)], LIM)
    for i in range(5, 8):
        local[i].wait()

    own_rows = pl.ds(pl.multiple_of(z * ROWS, ROWS), ROWS)
    current = x_ref[own_rows, :]

    for p in range(2):
        base = PASS + 6 * p
        if p == 1:
            for k in range(1, NY):
                put(ow_own, ow_own, OY, dev_y(k)[1]).start()
            w_q = jnp.concatenate([qw[i, j].reshape(256, 128) for i in range(4) for j in range(2)], axis=1)
            qz[z] = dot_nt(current, w_q).astype(BF) * jnp.asarray(0.125, BF)

            for k in FAR_FIRST:
                put(qz.at[z], qz.at[z], base + GQZ, dev_z(k)[1]).start()
            to_core(kvw, KVX, KVC)
            arrived(kvw.at[:, 0], KVC)
            w_pair = jnp.concatenate([kvw[i, j].reshape(512, 128) for i in range(4) for j in range(2)], axis=1)
            pair = dot_nt(current, w_pair)
            arrived(qz.at[pl.ds(0, NZ - 1)], base + GQZ)
            qt[1] = jnp.transpose(qz[...].reshape(TOK, 256)).reshape(NZ, 16, TOK)
        else:
            arrived(qt.at[p, pl.ds(0, NZ - 1)], base + GQZ)
            relay(up, UP)
            ff_to_x(up, UP, 0)
            spread(wq_ref, qw.at[x, c, lax.rem(z, 4), y], QZ, to_q)

        @pl.loop(0, NY)
        def _(j):
            if p == 0:
                @pl.when(j == 1)
                def _():
                    relay(down, DOWN)
                    ff_to_x(down, DOWN, 0)

            for i in range(2):
                keys = kvb[j, 0, :, :, 128 * i : 128 * i + 128].reshape(KEYS, 128)
                q_pair = qt[p, 8 * i : 8 * i + 8].reshape(2, 64, TOK)
                none = jnp.zeros((64, TOK), BF)
                both = jnp.concatenate(
                    [
                        jnp.concatenate([q_pair[0], none], axis=1),
                        jnp.concatenate([none, q_pair[1]], axis=1),
                    ],
                    axis=0,
                )
                scores = dot_nn(keys, both)
                offsets = lax.broadcasted_iota(jnp.int32, (128, 2 * TOK), 0).astype(F32)
                masked = jnp.concatenate(
                    [
                        jnp.where(
                            offsets < jnp.concatenate([lim[j, n : n + 1, :]] * 4, axis=1),
                            scores[128 * n : 128 * (n + 1)],
                            MASKED,
                        )
                        for n in range(3)
                    ],
                    axis=0,
                )
                peaks = jnp.maximum(jnp.max(masked, axis=0, keepdims=True), FLOOR_SCORE)
                weights = jnp.exp(masked - peaks).astype(BF)
                summed = dot_nn(vt[j, i], weights)
                po[j, 128 * i : 128 * i + 64, :] = summed[0:64, 0:TOK]
                po[j, 128 * i + 64 : 128 * i + 128, :] = summed[64:128, TOK : 2 * TOK]
                pm[j, 2 * i : 2 * i + 1, :] = peaks[:, 0:TOK]
                pm[j, 2 * i + 1 : 2 * i + 2, :] = peaks[:, TOK : 2 * TOK]
                pm[j, 4 + 2 * i : 5 + 2 * i, :] = summed[128:129, 0:TOK]
                pm[j, 5 + 2 * i : 6 + 2 * i, :] = summed[128:129, TOK : 2 * TOK]

        if p == 0:
            arrived(rkp.at[pl.ds(0, NZ - 1)], KPZ)
            pieces = [
                sum(pltpu.roll(rkp[4 * i + n].astype(F32), 32 * n, 1) for n in range(1, 4)) + rkp[4 * i].astype(F32)
                for i in range(4)
            ]
            pair = jnp.concatenate(pieces, axis=1)
        row_head = lax.div(lax.broadcasted_iota(jnp.int32, (64, 256), 0), 16)
        lane_head = lax.div(lax.broadcasted_iota(jnp.int32, (64, 256), 1), 64)
        own_head = row_head == lane_head
        k_block = jnp.where(own_head, jnp.concatenate([pair[:, 0:256]] * 4, axis=0), 0.0).astype(BF)
        v_block = jnp.where(own_head, jnp.concatenate([pair[:, 256:512]] * 4, axis=0), 0.0)
        b_scores = dot_nn(k_block, qt[p].reshape(256, TOK)).reshape(4, 16, TOK)
        b_peak = jnp.max(b_scores, axis=1)
        b_weights = jnp.exp(b_scores - b_peak[:, None, :]).astype(BF)
        b_total = jnp.sum(b_weights.astype(F32), axis=1)
        b_sum = dot_nn(jnp.transpose(v_block).astype(BF), b_weights.reshape(64, TOK))

        peaks_y = pm[:, 0:4, :]
        peak = jnp.maximum(jnp.max(peaks_y, axis=0), b_peak)
        scale = jnp.exp(peaks_y - peak[None])
        b_scale = jnp.exp(b_peak - peak)
        total = jnp.sum(scale * pm[:, 4:8, :], axis=0) + b_scale * b_total
        parts = []
        for h in range(4):
            rows = slice(64 * h, 64 * h + 64)
            value = b_sum[rows] * b_scale[h : h + 1]
            for i in range(NY):
                value += po[i, rows, :] * scale[i, h : h + 1]
            parts.append(value)
        tz[p] = jnp.transpose(jnp.concatenate(parts, axis=0)).astype(BF).reshape(NZ, ROWS, 256)
        both = jnp.concatenate([peak, total], axis=0)
        belongs = lax.broadcasted_iota(jnp.int32, (8, 128), 0) == lax.div(
            lax.broadcasted_iota(jnp.int32, (8, 128), 1), ROWS
        )
        steps = [pltpu.roll(both[:, 128 * i : 128 * i + 128], 0, 1, stride=ROWS, stride_axis=0) for i in range(2)]
        for i in range(NZ):
            moved = pltpu.roll(steps[i // 8], (128 - ROWS * (i % 8)) % 128, 1)
            tzm[p, i] = jnp.sum(jnp.where(belongs, moved, 0.0), axis=0, keepdims=True)

        for k in FAR_FIRST:
            zp, dev = dev_z(k)
            put(tzm.at[p, zp], rzm.at[p, z], base + RSZM, dev).start()
            put(tz.at[p, zp], rz.at[p, z], base + RSZ, dev).start()

        rz[p, z] = tz[p, z]
        rzm[p, z] = tzm[p, z]
        if p == 0:
            ff_to_x(up, UP, 1)
            ff_to_x(down, DOWN, 1)
            ff_to_core(up, UP, 0)
            ff_to_core(down, DOWN, 0)

        arrived(rzm.at[p, pl.ds(0, NZ - 1)], base + RSZM)
        stats = rzm[p].reshape(NZ, 128)
        scale_z = jnp.exp(stats - jnp.max(stats, axis=0, keepdims=True))
        share = scale_z / jnp.sum(scale_z * pltpu.roll(stats, 64, 1), axis=0, keepdims=True)
        share = jnp.transpose(jnp.concatenate([share, jnp.zeros((128 - NZ, 128), F32)], axis=0))
        arrived(rz.at[p, pl.ds(0, NZ - 1)], base + RSZ)
        if p == 0:
            spread(wkv_ref, kvw.at[x, c, za, zc, y], KVZ, to_kv)
            to_core(ow_own, OX, OC)
        lower = lax.broadcasted_iota(jnp.int32, (ROWS, 128), 1) < 64
        halves = [jnp.zeros((ROWS, 128), F32), jnp.zeros((ROWS, 128), F32)]
        for i in range(NZ):
            for n in range(2):
                low = jnp.broadcast_to(share[32 * n : 32 * n + 16, i : i + 1], (ROWS, 128))
                high = jnp.broadcast_to(share[32 * n + 16 : 32 * n + 32, i : i + 1], (ROWS, 128))
                halves[n] += jnp.where(lower, low, high) * rz[p, i, :, 128 * n : 128 * n + 128].astype(F32)
        att[p, y] = jnp.concatenate(halves, axis=1).astype(BF)
        for k in range(1, NY):
            put(att.at[p, y], att.at[p, y], base + GAY, dev_y(k)[1]).start()
        if p == 0:
            ff_to_core(up, UP, 1)
            arrived(ow.at[:, 0, 0], OC)
        arrived(att.at[p, pl.ds(0, 3)], base + GAY)

        heads = jnp.concatenate([att[p, i] for i in range(NY)], axis=1)
        if p == 0:
            w_o = jnp.concatenate([ow[i, j, y].reshape(256, 128) for i in range(4) for j in range(2)], axis=1)
            ob[y] = dot_nt(heads, w_o)
            for k in range(1, NY):
                put(ob.at[y], ob.at[y], base + GOY, dev_y(k)[1]).start()
            ff_to_core(down, DOWN, 1)
            arrived(qw.at[0, 0], QZ)
            to_x(qw, QX)
            arrived(ob.at[pl.ds(0, 3)], base + GOY)
            projected = jnp.concatenate([ob[i] for i in range(NY)], axis=1)
        else:
            arrived(ow.at[:, :, pl.ds(0, 3)], OY)
            w_o = jnp.concatenate([ow[i, j].reshape(D, 128) for i in range(4) for j in range(2)], axis=1)
            projected = dot_nt(heads, w_o)
        settled = layer_norm(current.astype(F32) + projected, ga_ref[...]).astype(BF)

        if p == 0:
            ff_ready(up, UP)
        w_u = jnp.concatenate([up[i, j].reshape(D, 128) for i in range(4) for j in range(2)], axis=1)
        product = dot_nt(settled, w_u)
        hidden = (0.5 * product * (1.0 + lax.erf(product * (0.5**0.5)))).astype(BF)
        if p == 0:
            ff_ready(down, DOWN)
        w_d = jnp.concatenate([down[i, j].reshape(D, 128) for i in range(4) for j in range(2)], axis=1)
        fp[p, y] = dot_nn(hidden, w_d).astype(BF)
        for k in range(1, NY):
            put(fp.at[p, y], fp.at[p, y], base + RFY, dev_y(k)[1]).start()
        if p == 0:
            to_core(qw, QX, QC)
            arrived(kvw.at[0, 0], KVZ)
            to_x(kvw, KVX)
            arrived(qw.at[:, 0], QC)
        arrived(fp.at[p, pl.ds(0, 3)], base + RFY)
        projected = fp[p, 0].astype(F32) + fp[p, 1].astype(F32) + fp[p, 2].astype(F32) + fp[p, 3].astype(F32)
        finished = layer_norm(settled.astype(F32) + projected, gm_ref[...])
        own_token = lax.broadcasted_iota(jnp.int32, (ROWS, TOK), 1) == z * ROWS + lax.broadcasted_iota(
            jnp.int32, (ROWS, TOK), 0
        )
        taken = jnp.sum(jnp.where(own_token, accept_ref[p].astype(F32), 0.0), axis=1, keepdims=True) > 0.5
        current = jnp.where(taken, finished, current.astype(F32)).astype(BF)

    fin[...] = current
    quarter = lanes(y * 256, 256)
    fz[z] = fin[:, quarter]

    def hand_on(zp):
        for k in range(1, NY):
            put(fz.at[zp], out_ref.at[zp, :, quarter], FIN_Y, dev_y(k)[1]).start()

    def in_turn(i):
        near = lax.div(i, 2) + 1
        return jnp.where(lax.rem(i, 2) == 0, near, NZ - near)

    @pl.loop(0, NZ - 1)
    def _(i):
        k = in_turn(i)
        put(fz.at[z], fz.at[z], FIN_Z + k, dev_z(k)[1]).start()

    hand_on(z)

    @pl.loop(0, NZ - 1)
    def _(i):
        k = in_turn(i)
        zp = lax.rem(z + NZ - k, NZ)
        arrived(fz.at[zp], FIN_Z + k)
        hand_on(zp)

    out_ref[:, :, quarter] = fz[...]
    arrived(out_ref.at[:, :, pl.ds(0, 768)], FIN_Y)

    def sent_but_own(ref, axis_end, ph, own):
        @pl.when(own)
        def _():
            sent(ref.at[pl.ds(0, axis_end - 1)], ph)

        @pl.when(jnp.logical_not(own))
        def _():
            sent(ref.at[pl.ds(0, axis_end)], ph)

    sent_but_own(ws, 8, WS, to_t == t)
    sent_but_own(qz, NZ, KVZ, to_kv == y)
    sent_but_own(hold, NZ, OZ, to_q == y)
    sent_but_own(hold, NZ, QZ, to_q == y)
    sent_but_own(ws2, 8, WS2, to_p == t)
    sent(rkp.at[pl.ds(0, NZ - 1)], KPZ)
    sent(ow.at[:, :, pl.ds(0, 3)], OY)
    for ref, xs, cs in ((qw, QX, QC), (kvw, KVX, KVC), (ow_own, OX, OC)):
        sent(ref.at[pl.ds(0, 3), 0], xs)
        sent(ref.at[:, 0], cs)
    for ph in (UP, DOWN):
        sent(up.at[0, 0, pl.ds(0, 8)], ph)
        sent(up.at[0, 0, pl.ds(0, 7)], ph + 3)
        for n in range(2):
            low, high = part(n)
            sent(up.at[pl.ds(0, 3), 0, pl.ds(0, high - low)], ph + 4 + n)
            sent(up.at[:, 0, pl.ds(0, high - low)], ph + 6 + n)
    for k in range(1, NY):
        sent(kvb.at[0], CY + k)
    sent(lim.at[pl.ds(0, 3)], LIM)
    for p in range(2):
        base = PASS + 6 * p
        sent(qz.at[pl.ds(0, NZ - 1)], base + GQZ)
        sent(rz.at[p, pl.ds(0, NZ - 1)], base + RSZ)
        sent(rzm.at[p, pl.ds(0, NZ - 1)], base + RSZM)
        sent(att.at[p, pl.ds(0, 3)], base + GAY)
        if p == 0:
            sent(ob.at[pl.ds(0, 3)], base + GOY)
        sent(fp.at[p, pl.ds(0, 3)], base + RFY)

    @pl.loop(1, NZ)
    def _(k):
        sent(fz.at[0], FIN_Z + k)

    sent(out_ref.at[:, :, pl.ds(0, 768)], FIN_Y)


def shards(
    block_in, accept, cache_len, slot_page, cache_kv, w_query, w_key_value, w_out, gain_attn, w_up, w_down, gain_mlp
):
    smem = pl.BlockSpec(memory_space=pltpu.SMEM)
    result = pl.pallas_call(
        kernel,
        out_shape=jax.ShapeDtypeStruct((NZ, ROWS, D), BF),
        in_specs=[smem, smem] + [pl.BlockSpec(memory_space=pltpu.HBM)] * 10,
        out_specs=pl.BlockSpec(memory_space=pltpu.VMEM),
        scratch_shapes=[
            pltpu.VMEM((TOK, D), BF),
            pltpu.VMEM((2, 1, TOK), jnp.int32),
            pltpu.VMEM((1, D), F32),
            pltpu.VMEM((1, D), F32),
            pltpu.VMEM((NY, 2, 3, 128, 256), BF),
            pltpu.VMEM((NY, 2, 144, KEYS), BF),
            pltpu.VMEM((NY, 8, 128), F32),
            pltpu.VMEM((8, 16, 128), BF),
            pltpu.VMEM((8, 32, 128), BF),
            pltpu.VMEM((NZ, ROWS, 128), BF),
            pltpu.VMEM((NZ, ROWS, 128), BF),
            pltpu.VMEM((4, 2, 4, 4, 16, 128), BF),
            pltpu.VMEM((4, 2, 2, 2, 4, 32, 128), BF),
            pltpu.VMEM((4, 2, NY, 4, 4, 16, 128), BF),
            pltpu.VMEM((4, 2, NZ, 64, 128), BF),
            pltpu.VMEM((4, 2, NZ, 64, 128), BF),
            pltpu.VMEM((NZ, 16, 128), BF),
            pltpu.VMEM((NZ, ROWS, 256), BF),
            pltpu.VMEM((2, NZ, 16, TOK), BF),
            pltpu.VMEM((NY, 256, TOK), F32),
            pltpu.VMEM((NY, 8, TOK), F32),
            pltpu.VMEM((2, NZ, ROWS, 256), BF),
            pltpu.VMEM((2, NZ, 1, 128), F32),
            pltpu.VMEM((2, NZ, ROWS, 256), BF),
            pltpu.VMEM((2, NZ, 1, 128), F32),
            pltpu.VMEM((2, NY, ROWS, 256), BF),
            pltpu.VMEM((NY, ROWS, 256), F32),
            pltpu.VMEM((2, NY, ROWS, D), BF),
            pltpu.VMEM((ROWS, D), BF),
            pltpu.VMEM((NZ, ROWS, 256), BF),
            pltpu.SemaphoreType.DMA((N_SEM,)),
            pltpu.SemaphoreType.DMA((N_SEM,)),
            pltpu.SemaphoreType.DMA((8,)),
        ],
        compiler_params=pltpu.CompilerParams(
            collective_id=0, has_side_effects=True, vmem_limit_bytes=63 * 1024 * 1024
        ),
    )(
        cache_len,
        slot_page,
        block_in[0],
        accept,
        cache_kv[0],
        w_query.T,
        w_key_value.T,
        w_out.T,
        w_up.T,
        w_down,
        gain_attn[None],
        gain_mlp[None],
    )
    return result.reshape(1, TOK, D)


def solution(mesh):
    in_specs = (
        P("seq", None, None),
        P(None, "seq", None),
        P("seq"),
        P("seq", "tok"),
        P("seq", "tok", None, None),
        P("seq", "tok"),
        P("seq", "tok"),
        P("seq", "tok"),
        P(),
        P("seq", "tok"),
        P("tok", "seq"),
        P(),
    )
    out_specs = P("seq", None, None)
    return jax.shard_map(shards, mesh=mesh, in_specs=in_specs, out_specs=out_specs, check_vma=False)
```
